512 devices in a mesh: gx: 32 (over z, x_lo), gy: 16 (over x_hi, y, core).
Axes of the slice: x: 4 (x_hi: 2, x_lo: 2; x = x_hi * 2 + x_lo), y: 4, z: 16, core: 2. Of those that a mesh axis runs over, the one named last changes fastest.
Arguments:
- positions: float32 [32, 16, 3, 128], P('gx', 'gy'), may hold values from 0 to 29
- species: int32 [32, 16, 128], P('gx', 'gy'), may hold values from 0 to 4
- senders: int32 [32, 16, 3, 128], P('gx', 'gy'), may hold values from 0 to 639, as said below
- counts: int32 [32, 16, 128], P('gx', 'gy'), may hold values from 1 to 3, as said below
- owners: int32 [32, 16, 3, 128], P('gx', 'gy'), may hold values 0 or 1
- send_list: int32 [32, 16, 64], P('gx', 'gy'), may hold values from 0 to 127, as said below
- embedding: float32 [128, 5], replicated, may hold values from -6 to 6
- radial_in_one: float32 [64, 8], replicated, may hold values from -2 to 2
- radial_mid_one: float32 [64, 64], replicated, may hold values from -0.75 to 0.75
- radial_out_one: float32 [384, 64], replicated, may hold values from -0.75 to 0.75
- mixing: float32 [3, 128, 128], replicated, may hold values from -0.5 to 0.5
- square_mix: float32 [128, 128], replicated, may hold values from -0.5 to 0.5
- readout_one: float32 [128], replicated, may hold values from -0.5 to 0.5
- radial_in_two: float32 [64, 8], replicated, may hold values from -2 to 2
- radial_mid_two: float32 [64, 64], replicated, may hold values from -0.75 to 0.75
- radial_out_two: float32 [384, 64], replicated, may hold values from -0.75 to 0.75
- mix_two: float32 [128, 128], replicated, may hold values from -0.5 to 0.5
- read_hidden: float32 [16, 128], replicated, may hold values from -0.5 to 0.5
- read_out: float32 [16], replicated, may hold values from -1.5 to 1.5
Outputs:
- forces: float32 [32, 16, 3, 128], P('gx', 'gy')
- energies: float32 [32, 16, 128], P('gx', 'gy')
The draws below stay inside these ranges and needn't reach their ends.
Inputs may be any that keep to these rules, and one draw needn't show every extreme that they name: `counts`: every atom has at least one live slot, and some atom of every domain has all 3 slots live. `send_list`: each domain's list holds 64 distinct atoms of that domain. `senders`: an atom's slots name distinct atoms other than itself. Atom n of a domain sits at lattice site ((n // 2) // 8, (n // 2) % 8, n % 2); a ghost taken from the domain at offset (i - 1, j - 1) sits at its own site in that domain plus ((i - 1) * 8, (j - 1) * 8, 0). The site of every atom that a slot names differs from the site of the slot's atom by at most one along each of the three dimensions.
All inputs are finite; a program needn't handle non-finite values. No bound on the sum of `owners` on one device may be relied on, other than what follows from the above.
Results may differ from the reference program's by a relative error of at most 0.0003.
Values sent between devices are 32-bit elements; how exact they have to be, the bound alone decides.
No kernel may reach another device: no remote copies, remote signals or barrier semaphores. Data moves between devices by JAX's collectives and lax.ppermute only.
A program may use at most 64 MiB of HBM per device.

```python
import math
import jax
import jax.numpy as jnp
from jax import lax

CH = 128
RADIAL = 64
NBASIS = 8
READ = 16
SPECIES = 5
NEIGH = 3
SIDE = 8
LAYERS = 2
ATOMS_DEV = 128
BOUND_DEV = 64
GRID_X = 32
GRID_Y = 16


def lattice_sites():
    atom_index = jnp.arange(SIDE * SIDE * LAYERS)
    column = atom_index // LAYERS
    return (column // SIDE, column % SIDE, atom_index % LAYERS, atom_index)


def ghost_plan(key):
    lattice_key = jax.random.fold_in(key, 7)
    score_key, order_key = jax.random.split(lattice_key)
    site_x, site_y, site_z, atom_index = lattice_sites()
    atoms = SIDE * SIDE * LAYERS
    domains = GRID_X * GRID_Y
    on_edge = ((site_x == 0) | (site_x == SIDE - 1) | (site_y == 0) | (site_y == SIDE - 1)).astype(jnp.int32)
    noise_bits = jax.random.randint(score_key, (domains, atoms), 0, 1 << 16)
    scores = (noise_bits + on_edge[None, :] * (1 << 16)) * atoms + atom_index[None, :]
    top_values, chosen = lax.top_k(scores, BOUND_DEV)
    order_keys = jax.random.split(order_key, domains)
    shuffled = jax.vmap(lambda single, picked: picked[jax.random.permutation(single, BOUND_DEV)])(order_keys, chosen)
    inverse = jax.vmap(lambda picked: jnp.zeros((atoms,), jnp.int32).at[picked].set(jnp.arange(BOUND_DEV).astype(jnp.int32)))(shuffled)
    return (shuffled.astype(jnp.int32), inverse)


def draw_send_list(key, part):
    shuffled, inverse = ghost_plan(key)
    return shuffled.reshape(GRID_X, GRID_Y, BOUND_DEV).astype(jnp.int32)


def draw_senders(key, part):
    shuffled, inverse = ghost_plan(key)
    site_x, site_y, site_z, atom_index = lattice_sites()
    atoms = SIDE * SIDE * LAYERS
    domains = GRID_X * GRID_Y
    offsets = jnp.arange(27)
    step_x = offsets // 9 - 1
    step_y = offsets // 3 % 3 - 1
    step_z = offsets % 3 - 1
    target_z = site_z[:, None] + step_z[None, :]
    usable = (target_z >= 0) & (target_z < LAYERS) & (offsets[None, :] != 13)
    noise_bits = jax.random.randint(jax.random.fold_in(key, 13), (domains, atoms, 27), 0, 1 << 16)
    scores = jnp.where(usable[None], noise_bits * 32 + offsets[None, None, :], -1)
    top_values, picked = lax.top_k(scores, NEIGH)
    target_x = site_x[None, :, None] + step_x[picked]
    target_y = site_y[None, :, None] + step_y[picked]
    target_layer = site_z[None, :, None] + step_z[picked]
    block_x = (target_x >= 0).astype(jnp.int32) + (target_x >= SIDE).astype(jnp.int32)
    block_y = (target_y >= 0).astype(jnp.int32) + (target_y >= SIDE).astype(jnp.int32)
    wrapped = (target_x % SIDE * SIDE + target_y % SIDE) * LAYERS + target_layer
    domain_ids = jnp.arange(domains)
    first_at = (domain_ids // GRID_Y)[:, None, None]
    second_at = (domain_ids % GRID_Y)[:, None, None]
    owner_domain = (first_at + block_x - 1) % GRID_X * GRID_Y + (second_at + block_y - 1) % GRID_Y
    slot_place = inverse[owner_domain, wrapped]
    block_id = 3 * block_x + block_y
    compact = block_id - (block_id > 4).astype(jnp.int32)
    ghost_index = atoms + compact * BOUND_DEV + slot_place
    sender = jnp.where(block_id == 4, wrapped, ghost_index)
    return jnp.moveaxis(sender.reshape(GRID_X, GRID_Y, atoms, NEIGH), 3, 2).astype(jnp.int32)


def draw_positions(key, part):
    site_x, site_y, site_z, atom_index = lattice_sites()
    atoms = SIDE * SIDE * LAYERS
    lattice = jnp.stack([(site_x.astype(jnp.float32) + 0.5) * 1.75, (site_y.astype(jnp.float32) + 0.5) * 1.75, (site_z.astype(jnp.float32) + 0.5) * 3.25])
    widths = jnp.array([1.75, 1.75, 3.25], jnp.float32)[:, None]
    jitter_key = jax.random.fold_in(key, 5)
    jitter = jax.random.uniform(jitter_key, (GRID_X, GRID_Y, 3, atoms), minval=-0.25, maxval=0.25)
    return (lattice[None, None] + jitter * widths[None, None]).astype(jnp.float32)


def draw_counts(key, part):
    count_key = jax.random.fold_in(key, 11)
    dense_key, bits_key, pick_key = jax.random.split(count_key, 3)
    dense_flag = jax.random.randint(dense_key, (GRID_X, GRID_Y, 1), 0, 2)
    lowest = jnp.where(dense_flag == 1, NEIGH // 2, 1)
    lowest = jnp.maximum(lowest, 1)
    raw_bits = jax.random.randint(bits_key, (GRID_X, GRID_Y, ATOMS_DEV), 0, 1 << 20)
    counts = lowest + raw_bits % (NEIGH + 1 - lowest)
    chosen = jax.random.randint(pick_key, (GRID_X, GRID_Y, 1), 0, ATOMS_DEV)
    atom_iota = jnp.arange(ATOMS_DEV)[None, None, :]
    return jnp.where(atom_iota == chosen, NEIGH, counts).astype(jnp.int32)


def with_ends(values, own_key, least, largest):
    index_at = [jax.random.randint(jax.random.fold_in(own_key, axis), (), 0, length) for axis, length in enumerate(values.shape)]
    main_axis = values.shape.index(max(values.shape))
    next_to = index_at[:main_axis] + [(index_at[main_axis] + 1) % values.shape[main_axis]] + index_at[main_axis + 1:]
    return values.at[tuple(index_at)].set(least).at[tuple(next_to)].set(largest)


def centred(rng, shape, scale, limit, dtype=jnp.bfloat16):
    values = jax.random.normal(rng, shape, jnp.float32) * scale
    return jnp.minimum(jnp.maximum(values, -limit), limit).astype(dtype)


def setup_inputs(seed: int = 0) -> dict:
    key_of = jax.random.split(jax.random.key(seed), 20)
    return {
        "positions": draw_positions(jax.random.fold_in(key_of[19], 71), 0),
        "species": with_ends(jax.random.randint(key_of[1], (GRID_X, GRID_Y, ATOMS_DEV), 0, SPECIES), jax.random.fold_in(key_of[1], 1), 0, SPECIES - 1).astype(jnp.int32),
        "senders": draw_senders(jax.random.fold_in(key_of[19], 71), 0),
        "counts": draw_counts(jax.random.fold_in(key_of[19], 71), 0),
        "owners": with_ends((jax.random.randint(key_of[4], (GRID_X, GRID_Y, NEIGH, ATOMS_DEV), 0, 2) < 1).astype(jnp.int32), jax.random.fold_in(key_of[4], 1), 0, 1),
        "send_list": draw_send_list(jax.random.fold_in(key_of[19], 71), 0),
        "embedding": centred(key_of[6], (CH, SPECIES), 1.0, 6.0, jnp.float32),
        "radial_in_one": centred(key_of[7], (RADIAL, NBASIS), NBASIS ** -0.5, 2.0, jnp.float32),
        "radial_mid_one": centred(key_of[8], (RADIAL, RADIAL), RADIAL ** -0.5, 0.75, jnp.float32),
        "radial_out_one": centred(key_of[9], (3 * CH, RADIAL), RADIAL ** -0.5, 0.75, jnp.float32),
        "mixing": centred(key_of[10], (3, CH, CH), CH ** -0.5, 0.5, jnp.float32),
        "square_mix": centred(key_of[11], (CH, CH), CH ** -0.5, 0.5, jnp.float32),
        "readout_one": centred(key_of[12], (CH,), CH ** -0.5, 0.5, jnp.float32),
        "radial_in_two": centred(key_of[13], (RADIAL, NBASIS), NBASIS ** -0.5, 2.0, jnp.float32),
        "radial_mid_two": centred(key_of[14], (RADIAL, RADIAL), RADIAL ** -0.5, 0.75, jnp.float32),
        "radial_out_two": centred(key_of[15], (3 * CH, RADIAL), RADIAL ** -0.5, 0.75, jnp.float32),
        "mix_two": centred(key_of[16], (CH, CH), CH ** -0.5, 0.5, jnp.float32),
        "read_hidden": centred(key_of[17], (READ, CH), CH ** -0.5, 0.5, jnp.float32),
        "read_out": centred(key_of[18], (READ,), READ ** -0.5, 1.5, jnp.float32),
    }


precise = lax.Precision.HIGHEST
spacing = 1.75
cutoff = 5.0
soften = 0.25
pair_strength = 2.0

def product(left_side, right_side):
    return jnp.dot(left_side, right_side, precision=precise, preferred_element_type=jnp.float32)

def harmonics(direction):
    along_x = direction[0]
    along_y = direction[1]
    along_z = direction[2]
    root_three = math.sqrt(3.0)
    root_five = math.sqrt(5.0)
    root_fifteen = math.sqrt(15.0)
    return jnp.stack([jnp.ones_like(along_x), root_three * along_x, root_three * along_y, root_three * along_z, root_fifteen * along_x * along_y, root_fifteen * along_y * along_z, 0.5 * root_five * (2.0 * along_z * along_z - along_x * along_x - along_y * along_y), root_fifteen * along_x * along_z, 0.5 * root_fifteen * (along_x * along_x - along_y * along_y)])

def geometry(places, ghost_places, table_index, basis_count):
    places_all = jnp.concatenate([places, ghost_places], axis=1)
    repeats = table_index.shape[0] // places.shape[1]
    displace = places_all[:, table_index] - jnp.tile(places, (1, repeats))
    radius = jnp.sqrt(lax.optimization_barrier(jnp.sum(displace * displace, axis=0)) + soften)
    direction = displace / radius
    scaled_radius = jnp.minimum(radius / cutoff, 1.0)
    envelope = 1.0 - 28.0 * scaled_radius ** 6 + 48.0 * scaled_radius ** 7 - 21.0 * scaled_radius ** 8
    orders = jnp.arange(1, basis_count + 1).astype(jnp.float32)[:, None]
    radial_basis = math.sqrt(2.0 / cutoff) * jnp.sin(orders * math.pi * scaled_radius) / radius * envelope
    return (harmonics(direction), radial_basis, envelope, radius)

def radial(radial_basis, weight_in, weight_mid, weight_out):
    hidden = jax.nn.silu(product(weight_in, radial_basis))
    hidden = jax.nn.silu(product(weight_mid, hidden))
    return product(weight_out, hidden)

def flat_index(senders, atom_count, bound_count):
    ghost_slot = senders - atom_count
    blocks_of = ghost_slot // bound_count
    blocks_of = blocks_of + (blocks_of >= 4).astype(jnp.int32)
    spot = atom_count + blocks_of * bound_count + ghost_slot % bound_count
    return jnp.where(senders < atom_count, senders, spot).reshape(-1).astype(jnp.int32)

def live_slots(counts, slot_count):
    return (jnp.arange(slot_count)[:, None] < counts[None, :]).astype(jnp.float32).reshape(-1)

def ghost_shift(bound_count):
    blocks_of = jnp.arange(9 * bound_count) // bound_count
    side_length = spacing * SIDE
    shift_x = (blocks_of // 3 - 1).astype(jnp.float32) * side_length
    shift_y = (blocks_of % 3 - 1).astype(jnp.float32) * side_length
    return jnp.stack([shift_x, shift_y, jnp.zeros_like(shift_x)])

def layer_one(places, ghost_places, embedded, ghost_embedded, table_index, live_mask, owner_mask, weight_in, weight_mid, weight_out, mixing, square_mix, readout_one):
    shapes, radial_basis, envelope, radius = geometry(places, ghost_places, table_index, weight_in.shape[1])
    atom_count = places.shape[1]
    channels = embedded.shape[0]
    slot_count = table_index.shape[0] // atom_count
    edge_weight = radial(radial_basis, weight_in, weight_mid, weight_out).reshape(3, channels, -1)
    sender_rows = jnp.concatenate([embedded, ghost_embedded], axis=1)[:, table_index]
    carried = (edge_weight * (sender_rows * live_mask)[None]).reshape(3, channels, slot_count, atom_count)
    shaped = shapes.reshape(9, slot_count, atom_count)
    scalar_part = jnp.einsum('cna,na->ca', carried[0], shaped[0], precision=precise)[None]
    vector_part = jnp.einsum('cna,kna->kca', carried[1], shaped[1:4], precision=precise)
    tensor_part = jnp.einsum('cna,kna->kca', carried[2], shaped[4:9], precision=precise)
    moments = jnp.concatenate([scalar_part, vector_part, tensor_part], 0) / slot_count
    squares = lax.optimization_barrier(jnp.sum(moments * moments, axis=0))
    scalar_feature = product(mixing[0], moments[0]) + product(square_mix, squares) + embedded
    vectors = jnp.einsum('ij,kja->kia', mixing[1], moments[1:4], precision=precise)
    tensors = jnp.einsum('ij,kja->kia', mixing[2], moments[4:9], precision=precise)
    features = jnp.concatenate([scalar_feature[None], vectors, tensors], 0).reshape(9 * channels, atom_count)
    pair_energy = (owner_mask * live_mask * pair_strength * jnp.exp(-radius) * envelope).reshape(slot_count, atom_count).sum(0)
    energy = product(readout_one, scalar_feature) + pair_energy
    return (features, energy)

def layer_two(places, ghost_places, features, ghost_features, table_index, live_mask, weight_in, weight_mid, weight_out, mix_two, read_hidden, read_out):
    shapes, radial_basis, envelope, radius = geometry(places, ghost_places, table_index, weight_in.shape[1])
    atom_count = places.shape[1]
    channels = mix_two.shape[0]
    slot_count = table_index.shape[0] // atom_count
    edge_weight = radial(radial_basis, weight_in, weight_mid, weight_out).reshape(3, channels, -1)
    sender_rows = jnp.concatenate([features, ghost_features], axis=1)[:, table_index].reshape(9, channels, -1)
    projected = sender_rows * shapes[:, None, :]
    scalar = (edge_weight[0] * projected[0] + edge_weight[1] * lax.optimization_barrier(jnp.sum(projected[1:4], 0)) + edge_weight[2] * lax.optimization_barrier(jnp.sum(projected[4:9], 0))) * live_mask
    gathered = scalar.reshape(channels, slot_count, atom_count).sum(1) / slot_count
    refined = product(mix_two, gathered) + features[:channels]
    return product(read_out, jax.nn.silu(product(read_hidden, refined)))

def reference(positions, species, senders, counts, owners, send_list, embedding, radial_in_one, radial_mid_one, radial_out_one, mixing, square_mix, readout_one, radial_in_two, radial_mid_two, radial_out_two, mix_two, read_hidden, read_out):
    grid_x = positions.shape[0]
    grid_y = positions.shape[1]
    atom_count = positions.shape[3]
    bound_count = send_list.shape[2]
    slot_count = senders.shape[2]
    domains = grid_x * grid_y
    embedded_all = jnp.moveaxis(embedding[:, species], 0, 2)
    picker = send_list[:, :, None, :]
    bound_places = jnp.take_along_axis(positions, picker, axis=3)
    bound_embedded = jnp.take_along_axis(embedded_all, picker, axis=3)
    offsets = ghost_shift(bound_count)
    domain_ids = jnp.arange(domains).astype(jnp.int32)

    def beside_all(table, first_at, second_at):
        pieces = [table[(first_at + step_x - 1) % grid_x, (second_at + step_y - 1) % grid_y] for step_x in range(3) for step_y in range(3)]
        stacked = jnp.stack(pieces, 1)
        return stacked.reshape(stacked.shape[0], -1)

    def deposit(buffer, returned, first_at, second_at):
        pieces = returned.reshape(returned.shape[0], 9, bound_count)
        for step_x in range(3):
            for step_y in range(3):
                buffer = buffer.at[(first_at + step_x - 1) % grid_x, (second_at + step_y - 1) % grid_y].add(pieces[:, 3 * step_x + step_y])
        return buffer

    def unpack(domain):
        first_at = domain // grid_y
        second_at = domain % grid_y
        table_index = flat_index(senders[first_at, second_at], atom_count, bound_count)
        live_mask = live_slots(counts[first_at, second_at], slot_count)
        owner_mask = owners[first_at, second_at].astype(jnp.float32).reshape(-1)
        ghost_places = beside_all(bound_places, first_at, second_at) + offsets
        ghost_embedded = beside_all(bound_embedded, first_at, second_at)
        return (first_at, second_at, table_index, live_mask, owner_mask, ghost_places, ghost_embedded)

    def first_pass(domain):
        first_at, second_at, table_index, live_mask, owner_mask, ghost_places, ghost_embedded = unpack(domain)
        return layer_one(positions[first_at, second_at], ghost_places, embedded_all[first_at, second_at], ghost_embedded, table_index, live_mask, owner_mask, radial_in_one, radial_mid_one, radial_out_one, mixing, square_mix, readout_one)
    features_flat, energy_one = lax.map(first_pass, domain_ids)
    features_all = features_flat.reshape(grid_x, grid_y, -1, atom_count)
    feature_rows = features_all.shape[2]
    bound_features = jnp.take_along_axis(features_all, picker, axis=3)

    def second_pass(buffer, domain):
        first_at, second_at, table_index, live_mask, owner_mask, ghost_places, ghost_embedded = unpack(domain)
        ghost_features = beside_all(bound_features, first_at, second_at)

        def second_layer(place_arg, ghost_arg, feature_arg, ghost_feature_arg):
            return layer_two(place_arg, ghost_arg, feature_arg, ghost_feature_arg, table_index, live_mask, radial_in_two, radial_mid_two, radial_out_two, mix_two, read_hidden, read_out)
        energy_two, pullback = jax.vjp(second_layer, positions[first_at, second_at], ghost_places, features_all[first_at, second_at], ghost_features)
        grad_places, grad_ghosts, grad_features, grad_ghost_features = pullback(jnp.ones_like(energy_two))
        returned = jnp.concatenate([grad_ghost_features, grad_ghosts], 0)
        buffer = deposit(buffer, returned, first_at, second_at)
        return (buffer, (energy_two, grad_places, grad_features))
    buffer = jnp.zeros((grid_x, grid_y, feature_rows + 3, bound_count), jnp.float32)
    buffer, (energy_two, grad_places_two, grad_features_all) = lax.scan(second_pass, buffer, domain_ids)

    def third_pass(domain):
        first_at, second_at, table_index, live_mask, owner_mask, ghost_places, ghost_embedded = unpack(domain)
        back_rows = buffer[first_at, second_at]
        grad_features = grad_features_all[domain].at[:, send_list[first_at, second_at]].add(back_rows[:feature_rows])

        def first_layer(place_arg, ghost_arg):
            return layer_one(place_arg, ghost_arg, embedded_all[first_at, second_at], ghost_embedded, table_index, live_mask, owner_mask, radial_in_one, radial_mid_one, radial_out_one, mixing, square_mix, readout_one)
        outputs, pullback = jax.vjp(first_layer, positions[first_at, second_at], ghost_places)
        return pullback((grad_features, jnp.ones((atom_count,), jnp.float32)))
    grad_first, grad_ghost_first = lax.map(third_pass, domain_ids)

    def fourth_pass(place_buffer, domain):
        return (deposit(place_buffer, grad_ghost_first[domain], domain // grid_y, domain % grid_y), domain)
    place_buffer = jnp.zeros((grid_x, grid_y, 3, bound_count), jnp.float32)
    place_buffer, unused = lax.scan(fourth_pass, place_buffer, domain_ids)
    grad_total = (grad_first + grad_places_two).reshape(grid_x, grid_y, 3, atom_count)
    back_places = buffer[:, :, feature_rows:] + place_buffer

    def settle(grad_domain, back_domain, pick_rows):
        return grad_domain.at[:, pick_rows].add(back_domain)
    grad_total = jax.vmap(jax.vmap(settle))(grad_total, back_places, send_list)
    energies = (energy_one + energy_two).reshape(grid_x, grid_y, atom_count)
    return (-grad_total, energies)
```

```python
import math

import jax
import jax.numpy as jnp
import numpy as np
from jax import lax
from jax.experimental import pallas as pl
from jax.experimental.pallas import tpu as pltpu
from jax.sharding import PartitionSpec as P

SIDE = 8
SPACING = 1.75
CUTOFF = 5.0
SOFTEN = 0.25
STRENGTH = 2.0
F32 = jnp.float32
BF16 = jnp.bfloat16
INTERPRET = False

TILES = 11
EDGES = TILES * 128
EDGES_TWO = 7 * 128
EDGES_BACK = 6 * 128


def tables():
    lane = np.arange(128)
    site_x, site_y = lane // 16, lane // 2 % 8

    def outer(site):
        low = site >= 4
        return np.where(low, -1, 1), np.where(low, 8 - site, site + 1)

    block_x, ring_x = outer(site_x)
    block_y, ring_y = outer(site_y)
    none = np.zeros(128, np.int64)
    rings = np.concatenate([ring_x, ring_y, np.maximum(ring_x, ring_y)])
    blocks_x = np.concatenate([block_x, none, block_x])
    blocks_y = np.concatenate([none, block_y, block_y])
    source = np.concatenate([none, none + 1, none + 2])
    order = np.argsort(rings, kind="stable")
    atoms = np.zeros((8, 512), np.int64)
    atoms[0] = np.concatenate([lane, np.tile(lane, 3)[order]])
    atoms[1] = np.concatenate([none, source[order]])
    atoms[2] = np.concatenate([none, blocks_x[order]])
    atoms[3] = np.concatenate([none, blocks_y[order]])
    code = 3 * (atoms[2] + 1) + atoms[3] + 1
    atoms[4] = code
    atoms[5] = code * 192 + atoms[0]
    edges = np.zeros((8, EDGES), np.int64)
    tile_code = code.reshape(4, 128)
    edges[0] = np.concatenate(
        [tile_code[0]] * 3
        + [tile_code[1]] * 3
        + [tile_code[2][lane % 32]]
        + [tile_code[2]] * 3
        + [tile_code[3][lane % 8]]
    )
    two = np.where(lane < 96, lane // 32, 9)
    three = np.where(lane < 24, lane // 8, 9)
    slots = [none, none + 1, none + 2]
    edges[1] = np.concatenate(slots + slots + [two] + slots + [three])
    near = (lane < 72).astype(np.int64)
    edges[2] = np.concatenate([none + 1] * 3 + [near] * 3 + [none] * 5)
    return atoms.astype(np.int32), edges.astype(np.int32)


ATOM_TABLE, EDGE_TABLE = tables()


def rounded(x):
    return x.astype(BF16).astype(F32)


def split(x):
    high = x.astype(BF16)
    return high, (x - high.astype(F32)).astype(BF16)


def mm(a, b):
    return lax.dot_general(a, b, (((1,), (0,)), ((), ())), preferred_element_type=F32)


def mm_nt(a, b):
    return lax.dot_general(a, b, (((1,), (1,)), ((), ())), preferred_element_type=F32)


def dots(a, b):
    return mm(a[0], b[0]) + mm(a[0], b[1]) + mm(a[1], b[0])


def dot3(a, b):
    return dots(split(a), split(b))


def silu_pair(x):
    gate = 1.0 / (1.0 + jnp.exp(-x))
    return x * gate, gate * (1.0 + x * (1.0 - gate))


def lanes_from(x, index):
    return jnp.take_along_axis(x, index, axis=1, mode="promise_in_bounds")


def column_of(row, width=128):
    return jnp.broadcast_to(row, (width, row.shape[1])).T


def roll_up(x, amount):
    return pltpu.roll(x, 128 - amount, 1)


def pack_kernel(*refs):
    sources, out, copies, sems = refs[:6], refs[6], refs[7:13], refs[13]
    moves = [pltpu.make_async_copy(s, d, sems.at[i]) for i, (s, d) in enumerate(zip(sources, copies))]
    for move in moves:
        move.start()
    for move in moves:
        move.wait()
    pos, species, senders, counts, owners, send_list = copies
    for i in range(3):
        out[i : i + 1, :] = pos[i]
        out[4 + i : 5 + i, :] = senders[i].astype(F32)
        out[8 + i : 9 + i, :] = owners[i].astype(F32)
    out[3:4, :] = species[...].astype(F32)
    out[7:8, :] = counts[...].astype(F32)
    picked = jnp.broadcast_to(send_list[...].astype(F32), (128, 64)).T
    lane = lax.broadcasted_iota(jnp.int32, (64, 128), 1).astype(F32)
    row = lax.broadcasted_iota(jnp.int32, (64, 128), 0).astype(F32)
    slot = jnp.max(jnp.where(picked == lane, row, -1.0), axis=0, keepdims=True)
    out[11:16, :] = jnp.broadcast_to(slot, (5, 128))


def main_kernel(
    odd,
    mid,
    near_a,
    near_b,
    atom_table_hbm,
    edge_table_hbm,
    embedding_hbm,
    in_one_hbm,
    mid_one_hbm,
    out_one_hbm,
    mixing_hbm,
    square_mix_hbm,
    readout_one_hbm,
    in_two_hbm,
    mid_two_hbm,
    out_two_hbm,
    mix_two_hbm,
    read_hidden_hbm,
    read_out_hbm,
    forces,
    energies,
    hot0,
    hot1,
    hot2,
    emb_tab,
    spec_row,
    emb_edge,
    carried,
    shape_row,
    moments,
    squares,
    scalar_feat,
    feats,
    gathered_ref,
    proj,
    mix_split,
    mix_back,
    w_two,
    queue,
    square_grad,
    shape_grad,
    radial_grad,
    atom_table,
    edge_table,
    embedding,
    in_one,
    mid_one,
    out_one,
    mixing,
    square_mix,
    readout_one,
    in_two,
    mid_two,
    out_two,
    mix_two,
    read_hidden,
    read_out,
    sems,
):
    moves = [
        pltpu.make_async_copy(source, target, sems.at[i])
        for i, (source, target) in enumerate(
            (
                (atom_table_hbm, atom_table),
                (edge_table_hbm, edge_table),
                (embedding_hbm, embedding),
                (in_one_hbm, in_one),
                (mid_one_hbm, mid_one),
                (out_one_hbm, out_one),
                (mixing_hbm, mixing),
                (square_mix_hbm, square_mix),
                (readout_one_hbm, readout_one),
                (in_two_hbm, in_two),
                (mid_two_hbm, mid_two),
                (out_two_hbm, out_two),
                (mix_two_hbm, mix_two),
                (read_hidden_hbm, read_hidden),
                (read_out_hbm, read_out),
            )
        )
    ]
    for move in moves:
        move.start()
    moves[0].wait()
    moves[1].wait()
    lane256 = lax.broadcasted_iota(jnp.int32, (16, 256), 1) % 128
    from_a = (lane256 // 64) == odd[0]
    x_outer = jnp.where(from_a, near_a[...], near_b[...])
    own = mid[:, 0:128]
    sources = (x_outer[:, 0:128], mid[:, 128:256], x_outer[:, 128:256])
    row16 = lax.broadcasted_iota(jnp.int32, (16, 128), 0)
    atom_tiles = [own]
    key_b = []
    for t in range(4):
        cut = slice(128 * t, 128 * t + 128)
        if t:
            index = jnp.broadcast_to(atom_table[0:1, cut], (16, 128))
            which = jnp.broadcast_to(atom_table[1:2, cut], (16, 128))
            picked = [lanes_from(s, index) for s in sources]
            tile = jnp.where(which == 0, picked[0], jnp.where(which == 1, picked[1], picked[2]))
            block_x = jnp.broadcast_to(atom_table[2:3, cut].astype(F32), (16, 128))
            block_y = jnp.broadcast_to(atom_table[3:4, cut].astype(F32), (16, 128))
            shift = jnp.where(row16 == 0, block_x, jnp.where(row16 == 1, block_y, 0.0))
            atom_tiles.append(tile + shift * (SPACING * SIDE))
        slot = atom_tiles[t][11:12, :]
        code = atom_table[4:5, cut].astype(F32)
        key_b.append(jnp.where(slot < 0.0, -1.0, code * 192.0 + 128.0 + slot))
    lane16 = lax.broadcasted_iota(jnp.int32, (16, 128), 1)
    pack_two = lanes_from(atom_tiles[2], lane16 % 32)
    pack_three = lanes_from(atom_tiles[3], lane16 % 8)
    t0, t1, t2, t3 = atom_tiles
    receivers = jnp.concatenate([t0] * 3 + [t1] * 3 + [pack_two] + [t2] * 3 + [pack_three], 1)

    slot_row = edge_table[1:2, :]
    sent = jnp.where(
        slot_row == 0,
        receivers[4:5],
        jnp.where(slot_row == 1, receivers[5:6], receivers[6:7]),
    ).astype(jnp.int32)
    owned = jnp.where(
        slot_row == 0,
        receivers[8:9],
        jnp.where(slot_row == 1, receivers[9:10], receivers[10:11]),
    )
    live = (slot_row < receivers[7:8].astype(jnp.int32)).astype(F32)
    ghost = sent - 128
    block = lax.shift_right_arithmetic(ghost, 6)
    block = block + (block >= 4).astype(jnp.int32)
    code_row = edge_table[0:1, :]
    key = jnp.where(
        sent < 128,
        code_row * 192 + sent,
        (code_row + block - 4) * 192 + 128 + (ghost & 63),
    ).astype(F32)
    for c in range(4):
        cut = slice(128 * c, 128 * c + 128)
        plain = column_of(atom_table[5:6, cut].astype(F32))
        listed = column_of(key_b[c])
        for e in range(TILES):
            if e < 3 and c > 1:
                continue
            wanted = key[:, 128 * e : 128 * e + 128]
            hit = jnp.where((plain == wanted) | (listed == wanted), 1.0, 0.0).astype(BF16)
            if e < 3:
                hot0[cut, 128 * e : 128 * e + 128] = hit
            elif e < 7:
                hot1[cut, 128 * (e - 3) : 128 * (e - 3) + 128] = hit
            else:
                hot2[cut, 128 * (e - 7) : 128 * (e - 7) + 128] = hit

    raw = jnp.concatenate([t[0:8] for t in atom_tiles], 1)
    first = rounded(raw)
    second = rounded(raw - first)
    third = rounded(raw - first - second)
    terms = jnp.concatenate([first, second, third, third], 0).astype(BF16)
    found = jnp.concatenate(
        [mm(terms[:, 0:256], hot0[...]), mm(terms, hot1[...]), mm(terms, hot2[...])], 1
    )
    found = found[0:8] + found[8:16] + found[16:24]
    away = [found[i : i + 1] - receivers[i : i + 1] for i in range(3)]
    spec_row[0:1, :] = found[3:4]
    spec_row[1:2, :] = live

    radius_sq = away[0] * away[0] + away[1] * away[1] + away[2] * away[2] + SOFTEN
    radius = jnp.sqrt(radius_sq)
    inverse = 1.0 / radius
    ux, uy, uz = [a * inverse for a in away]
    scaled = jnp.minimum(radius / CUTOFF, 1.0)
    s2 = scaled * scaled
    s3 = s2 * scaled
    s6 = s3 * s3
    envelope = 1.0 - 28.0 * s6 + 48.0 * s6 * scaled - 21.0 * s6 * s2
    slope = jnp.where(radius < CUTOFF, 1.0 / CUTOFF, 0.0)
    gap = 1.0 - scaled
    envelope_slope = -168.0 * s3 * s2 * gap * gap * slope
    order = (lax.broadcasted_iota(jnp.int32, (8, EDGES), 0) + 1).astype(F32)
    phase = order * (math.pi * scaled)
    factor = math.sqrt(2.0 / CUTOFF)
    sines = factor * jnp.sin(phase)
    basis = sines * (envelope * inverse)
    near = slice(0, EDGES_BACK)
    cosines = factor * jnp.cos(phase[:, near])
    basis_slope = (
        order[:, near] * cosines * (math.pi * slope * envelope * inverse)[:, near]
        + sines[:, near] * ((envelope_slope - envelope * inverse) * inverse)[:, near]
    )
    r3, r5, r15 = math.sqrt(3.0), math.sqrt(5.0), math.sqrt(15.0)
    shape_row[0:9, :] = jnp.concatenate(
        [
            jnp.ones_like(ux),
            r3 * ux,
            r3 * uy,
            r3 * uz,
            r15 * ux * uy,
            r15 * uy * uz,
            (0.5 * r5) * (2.0 * uz * uz - ux * ux - uy * uy),
            r15 * ux * uz,
            (0.5 * r15) * (ux * ux - uy * uy),
        ],
        0,
    )
    pair = owned * live * STRENGTH * jnp.exp(-radius)
    pair_slope = (pair * (envelope_slope - envelope))[:, near]
    pair = pair * envelope
    pair_own = pair[:, 0:128] + pair[:, 128:256] + pair[:, 256:384]

    for move in moves[2:]:
        move.wait()
    for z in range(5):
        emb_tab[z] = column_of(embedding[z : z + 1, :])

    def element(code):
        value = emb_tab[0]
        for z in range(1, 5):
            value = jnp.where(code == float(z), emb_tab[z], value)
        return value

    def embed_edges(e, carry):
        at = pl.ds(pl.multiple_of(e * 128, 128), 128)
        emb_edge[:, at] = element(spec_row[0:1, at]) * spec_row[1:2, at]
        return carry

    lax.fori_loop(0, TILES, embed_edges, 0)

    basis_s = split(basis)
    pre1 = dots(split(in_one[...].T), basis_s)
    hid1, dhid1 = silu_pair(pre1)
    pre1 = dots(split(mid_one[...]), split(hid1))
    top1, dtop1 = silu_pair(pre1)
    dhid1, dtop1 = dhid1[:, near], dtop1[:, near]
    top1 = split(top1)
    for g in range(3):
        weight = dots(split(out_one[:, 128 * g : 128 * g + 128].T), top1)
        carried[g] = weight * emb_edge[...]
    basis_two = (basis_s[0][:, 0:EDGES_TWO], basis_s[1][:, 0:EDGES_TWO])
    pre2 = dots(split(in_two[...].T), basis_two)
    hid2, dhid2 = silu_pair(pre2)
    pre2 = dots(split(mid_two[...]), split(hid2))
    top2, dtop2 = silu_pair(pre2)
    dhid2, dtop2 = dhid2[:, near], dtop2[:, near]
    top2 = split(top2)
    for g in range(3):
        w_two[g] = dots(split(out_two[:, 128 * g : 128 * g + 128].T), top2)

    for g in range(3):
        high, low = split(mixing[g])
        mix_split[g, 0:128, :] = high
        mix_split[g, 128:256, :] = low
        high, low = split(mixing[g].T)
        mix_back[g, 0:128, :] = high
        mix_back[g, 128:256, :] = low

    def degree(m):
        return (m > 0).astype(jnp.int32) + (m > 3).astype(jnp.int32)

    def moment(m, g):
        y = shape_row[pl.ds(m, 1), :]

        def part(e):
            at = slice(128 * e, 128 * e + 128)
            return carried[g, :, at] * y[:, at]

        tail = part(10)
        value = jnp.concatenate(
            [
                part(0) + part(1) + part(2),
                part(3) + part(4) + part(5),
                part(7) + part(8) + part(9),
                tail + roll_up(tail, 8) + roll_up(tail, 16),
            ],
            1,
        ) * (1.0 / 3.0)
        moments[m] = value
        high, low = split(value)
        both = mm(mix_split[g], high)
        mixed = both[0:128] + both[128:256] + mm(mix_split[g, 0:128, :], low)
        return value, mixed

    value, mixed = moment(0, 0)
    squares[...] = value * value
    scalar_feat[...] = mixed

    def moment_step(m, carry):
        value, mixed = moment(m, degree(m))
        squares[...] += value * value
        high, low = split(mixed)
        feats[m, 0:128, :] = high
        feats[m, 128:256, :] = low
        return carry

    lax.fori_loop(1, 9, moment_step, 0)
    element_rows = jnp.concatenate([t[3:4] for t in atom_tiles], 1)
    scalar = scalar_feat[...] + dot3(square_mix[...], squares[...])
    scalar = scalar + jnp.concatenate(
        [element(element_rows[:, 128 * t : 128 * t + 128]) for t in range(4)], 1
    )
    scalar_feat[...] = scalar
    high, low = split(scalar)
    feats[0, 0:128, :] = high
    feats[0, 128:256, :] = low

    proj[...] = jnp.zeros_like(proj)

    def gather_step(m, carry):
        g = degree(m)
        left = feats[m]
        part = mm(left[:, 0:256], hot0[...])
        rest = mm(left, hot1[...])
        part = part[0:128] + part[128:256]
        rest = rest[0:128] + rest[128:256]
        gathered_ref[m, :, 0:384] = part
        gathered_ref[m, :, 384:896] = rest
        y = shape_row[pl.ds(m, 1), :]
        proj[g, :, 0:384] += part * y[:, 0:384]
        proj[g, :, 384:896] += rest * y[:, 384:896]
        return carry

    lax.fori_loop(0, 9, gather_step, 0)
    live_two = live[:, 0:EDGES_TWO]
    term = (w_two[0] * proj[0] + w_two[1] * proj[1] + w_two[2] * proj[2]) * live_two
    tail = term[:, 768:896]
    total = jnp.concatenate(
        [
            term[:, 0:128] + term[:, 128:256] + term[:, 256:384],
            term[:, 384:512] + term[:, 512:640] + term[:, 640:768],
            tail + roll_up(tail, 32) + roll_up(tail, 64),
        ],
        1,
    ) * (1.0 / 3.0)
    refined = dot3(mix_two[...], total) + scalar_feat[:, 0:384]
    hidden = dot3(read_hidden[...], refined)
    act, dact = silu_pair(hidden)
    out_column = jnp.broadcast_to(column_of(read_out[...])[:, 0:1], (16, 384))
    one_column = column_of(readout_one[...])
    energies[...] = (
        jnp.sum(act[:, 0:128] * out_column[:, 0:128], axis=0, keepdims=True)
        + jnp.sum(scalar_feat[:, 0:128] * one_column, axis=0, keepdims=True)
        + pair_own
    )

    refined_grad = dot3(read_hidden[...].T, dact * out_column)
    total_grad = dot3(mix_two[...].T, refined_grad) * (1.0 / 3.0)
    lane128 = lax.broadcasted_iota(jnp.int32, (128, 128), 1)
    tail = jnp.where(lane128 < 32, total_grad[:, 256:384], 0.0)
    tail = tail + pltpu.roll(tail, 32, 1) + pltpu.roll(tail, 64, 1)
    grad0, grad1 = total_grad[:, 0:128], total_grad[:, 128:256]
    term_grad = jnp.concatenate([grad0] * 3 + [grad1] * 3 + [tail], 1) * live_two
    for g in range(3):
        queue[g] = term_grad * w_two[g]
        proj[g, :, near] = term_grad[:, near] * proj[g, :, near]
    radial_grad[...] = jnp.zeros_like(radial_grad)

    def back(m, g, first):
        y = shape_row[pl.ds(m, 1), :]
        q = queue[g]
        high, low = split(q * y[:, 0:EDGES_TWO])
        left = jnp.concatenate([high, low], 0)
        grad = mm_nt(left[:, 0:384], hot0[...]) + mm_nt(left[:, 384:896], hot1[0:256, :])
        grad = grad[0:128] + grad[128:256]
        if first:
            grad = grad + refined_grad[:, 0:256] + jnp.concatenate([one_column] * 2, 1)
            square_grad[...] = 2.0 * dot3(square_mix[...].T, grad)
        high, low = split(grad)
        both = mm(mix_back[g], high)
        grad = both[0:128] + both[128:256] + mm(mix_back[g, 0:128, :], low)
        grad = (grad + square_grad[...] * moments[m, :, 0:256]) * (1.0 / 3.0)
        wide = jnp.concatenate([grad[:, 0:128]] * 3 + [grad[:, 128:256]] * 3, 1)
        both = q[:, near] * gathered_ref[m, :, near] + wide * carried[g, :, near]
        shape_grad[pl.ds(m, 1), :] = jnp.sum(both, axis=0, keepdims=True)
        radial_grad[g] += wide * y[:, near]

    back(0, 0, True)

    def back_step(m, carry):
        back(m, degree(m), False)
        return carry

    lax.fori_loop(1, 9, back_step, 0)

    def radial_back(grads, weight_out, weight_mid, weight_in, dtop, dhid):
        top_grad = 0.0
        for g in range(3):
            top_grad = top_grad + dot3(weight_out[:, 128 * g : 128 * g + 128], grads[g])
        hid_grad = dot3(weight_mid[...].T, top_grad * dtop)
        return dot3(weight_in[...], hid_grad * dhid)

    ones = [radial_grad[g] * emb_edge[:, near] for g in range(3)]
    basis_grad = radial_back(ones, out_one, mid_one, in_one, dtop1, dhid1)
    twos = [proj[g, :, near] for g in range(3)]
    basis_grad = basis_grad + radial_back(twos, out_two, mid_two, in_two, dtop2, dhid2)

    ux, uy, uz, inverse = ux[:, near], uy[:, near], uz[:, near], inverse[:, near]
    ym = [shape_grad[m : m + 1, :] for m in range(9)]
    gx = r3 * ym[1] + r15 * (uy * ym[4] + uz * ym[7] + ux * ym[8]) - r5 * ux * ym[6]
    gy = r3 * ym[2] + r15 * (ux * ym[4] + uz * ym[5] - uy * ym[8]) - r5 * uy * ym[6]
    gz = r3 * ym[3] + r15 * (uy * ym[5] + ux * ym[7]) + 2.0 * r5 * uz * ym[6]
    along = jnp.sum(basis_grad * basis_slope, axis=0, keepdims=True) + pair_slope
    along = along - (gx * ux + gy * uy + gz * uz) * inverse
    keep = edge_table[2:3, near].astype(F32)
    edge_grad = jnp.concatenate(
        [(gx * inverse + along * ux) * keep, (gy * inverse + along * uy) * keep,
         (gz * inverse + along * uz) * keep, jnp.zeros((5, EDGES_BACK), F32)],
        0,
    )
    high = rounded(edge_grad)
    left = jnp.concatenate([high, edge_grad - high], 0).astype(BF16)
    pulled = mm_nt(left[:, 0:384], hot0[0:128, :]) + mm_nt(left[:, 384:768], hot1[0:128, 0:384])
    pulled = pulled[0:8] + pulled[8:16]
    mine = edge_grad[:, 0:128] + edge_grad[:, 128:256] + edge_grad[:, 256:384]
    total = mine - pulled
    for i in range(3):
        forces[i] = total[i : i + 1]


def swap(value, axis, odd):
    count = lax.axis_size(axis)
    pairs = [(i, (((i - odd) ^ 1) + odd) % count) for i in range(count)]
    return lax.ppermute(value, axis, pairs)


def local(
    positions,
    species,
    senders,
    counts,
    owners,
    send_list,
    embedding,
    radial_in_one,
    radial_mid_one,
    radial_out_one,
    mixing,
    square_mix,
    readout_one,
    radial_in_two,
    radial_mid_two,
    radial_out_two,
    mix_two,
    read_hidden,
    read_out,
):
    packed = pl.pallas_call(
        pack_kernel,
        out_shape=jax.ShapeDtypeStruct((16, 128), F32),
        in_specs=[pl.BlockSpec(memory_space=pltpu.HBM)] * 6,
        out_specs=pl.BlockSpec(memory_space=pltpu.VMEM),
        scratch_shapes=[
            pltpu.VMEM((3, 1, 128), F32),
            pltpu.VMEM((1, 128), jnp.int32),
            pltpu.VMEM((3, 1, 128), jnp.int32),
            pltpu.VMEM((1, 128), jnp.int32),
            pltpu.VMEM((3, 1, 128), jnp.int32),
            pltpu.VMEM((1, 64), jnp.int32),
            pltpu.SemaphoreType.DMA((6,)),
        ],
        interpret=INTERPRET,
    )(
        positions.reshape(3, 1, 128),
        species[0],
        senders.reshape(3, 1, 128),
        counts[0],
        owners.reshape(3, 1, 128),
        send_list[0],
    )
    near_a, near_b = swap(packed, "gy", 0), swap(packed, "gy", 1)
    odd_y = lax.axis_index("gy") % 2
    lane = lax.broadcasted_iota(jnp.int32, (16, 128), 1)
    outer = jnp.where(lane // 8 % 2 == odd_y, near_a, near_b)
    mid = jnp.concatenate([packed, outer], 1)
    near_a, near_b = swap(mid, "gx", 0), swap(mid, "gx", 1)
    odd_x = (lax.axis_index("gx") % 2).astype(jnp.int32).reshape(1)
    held = (
        jnp.asarray(ATOM_TABLE),
        jnp.asarray(EDGE_TABLE),
        embedding.T,
        radial_in_one.T,
        radial_mid_one,
        radial_out_one.T,
        mixing,
        square_mix,
        readout_one.reshape(1, -1),
        radial_in_two.T,
        radial_mid_two,
        radial_out_two.T,
        mix_two,
        read_hidden,
        read_out.reshape(1, -1),
    )
    vmem = pl.BlockSpec(memory_space=pltpu.VMEM)
    forces, energies = pl.pallas_call(
        main_kernel,
        out_shape=(
            jax.ShapeDtypeStruct((3, 1, 128), F32),
            jax.ShapeDtypeStruct((1, 128), F32),
        ),
        in_specs=[pl.BlockSpec(memory_space=pltpu.SMEM)]
        + [vmem] * 3
        + [pl.BlockSpec(memory_space=pltpu.HBM)] * len(held),
        out_specs=(vmem, vmem),
        scratch_shapes=[
            pltpu.VMEM((256, 384), BF16),
            pltpu.VMEM((512, 512), BF16),
            pltpu.VMEM((512, 512), BF16),
            pltpu.VMEM((5, 128, 128), F32),
            pltpu.VMEM((8, EDGES), F32),
            pltpu.VMEM((128, EDGES), F32),
            pltpu.VMEM((3, 128, EDGES), F32),
            pltpu.VMEM((16, EDGES), F32),
            pltpu.VMEM((9, 128, 512), F32),
            pltpu.VMEM((128, 512), F32),
            pltpu.VMEM((128, 512), F32),
            pltpu.VMEM((9, 256, 512), BF16),
            pltpu.VMEM((9, 128, EDGES_TWO), F32),
            pltpu.VMEM((3, 128, EDGES_TWO), F32),
            pltpu.VMEM((3, 256, 128), BF16),
            pltpu.VMEM((3, 256, 128), BF16),
            pltpu.VMEM((3, 128, EDGES_TWO), F32),
            pltpu.VMEM((3, 128, EDGES_TWO), F32),
            pltpu.VMEM((128, 256), F32),
            pltpu.VMEM((16, EDGES_BACK), F32),
            pltpu.VMEM((3, 128, EDGES_BACK), F32),
        ]
        + [pltpu.VMEM(h.shape, h.dtype) for h in held]
        + [pltpu.SemaphoreType.DMA((len(held),))],
        interpret=INTERPRET,
    )(odd_x, mid, near_a, near_b, *held)
    return forces.reshape(1, 1, 3, 128), energies[None]


def solution(mesh):
    split_four = P("gx", "gy", None, None)
    split_three = P("gx", "gy", None)
    placed = (split_four, split_three, split_four, split_three, split_four, split_three)
    return jax.shard_map(
        local,
        mesh=mesh,
        in_specs=placed + (P(),) * 13,
        out_specs=(split_four, split_three),
        check_vma=False,
    )
```

```python
import math

import jax
import jax.numpy as jnp
import numpy as np
from jax import lax
from jax.experimental import pallas as pl
from jax.experimental.pallas import tpu as pltpu
from jax.sharding import PartitionSpec as P

SIDE = 8
SPACING = 1.75
CUTOFF = 5.0
SOFTEN = 0.25
STRENGTH = 2.0
F32 = jnp.float32
BF16 = jnp.bfloat16
INTERPRET = False

TILES = 11
EDGES = TILES * 128
EDGES_TWO = 7 * 128
EDGES_BACK = 6 * 128


def tables():
    lane = np.arange(128)
    site_x, site_y = lane // 16, lane // 2 % 8

    def outer(site):
        low = site >= 4
        return np.where(low, -1, 1), np.where(low, 8 - site, site + 1)

    block_x, ring_x = outer(site_x)
    block_y, ring_y = outer(site_y)
    none = np.zeros(128, np.int64)
    rings = np.concatenate([ring_x, ring_y, np.maximum(ring_x, ring_y)])
    blocks_x = np.concatenate([block_x, none, block_x])
    blocks_y = np.concatenate([none, block_y, block_y])
    source = np.concatenate([none, none + 1, none + 2])
    order = np.argsort(rings, kind="stable")
    atoms = np.zeros((8, 512), np.int64)
    atoms[0] = np.concatenate([lane, np.tile(lane, 3)[order]])
    atoms[1] = np.concatenate([none, source[order]])
    atoms[2] = np.concatenate([none, blocks_x[order]])
    atoms[3] = np.concatenate([none, blocks_y[order]])
    code = 3 * (atoms[2] + 1) + atoms[3] + 1
    atoms[4] = code
    atoms[5] = code * 192 + atoms[0]
    edges = np.zeros((8, EDGES), np.int64)
    tile_code = code.reshape(4, 128)
    edges[0] = np.concatenate(
        [tile_code[0]] * 3
        + [tile_code[1]] * 3
        + [tile_code[2][lane % 32]]
        + [tile_code[2]] * 3
        + [tile_code[3][lane % 8]]
    )
    two = np.where(lane < 96, lane // 32, 9)
    three = np.where(lane < 24, lane // 8, 9)
    slots = [none, none + 1, none + 2]
    edges[1] = np.concatenate(slots + slots + [two] + slots + [three])
    near = (lane < 72).astype(np.int64)
    edges[2] = np.concatenate([none + 1] * 3 + [near] * 3 + [none] * 5)
    return atoms.astype(np.int32), edges.astype(np.int32)


ATOM_TABLE, EDGE_TABLE = tables()


def rounded(x):
    return x.astype(BF16).astype(F32)


def split(x):
    high = x.astype(BF16)
    return high, (x - high.astype(F32)).astype(BF16)


def mm(a, b):
    return lax.dot_general(a, b, (((1,), (0,)), ((), ())), preferred_element_type=F32)


def mm_nt(a, b):
    return lax.dot_general(a, b, (((1,), (1,)), ((), ())), preferred_element_type=F32)


def dots(a, b):
    return mm(a[0], b[0]) + mm(a[0], b[1]) + mm(a[1], b[0])


def dot3(a, b):
    return dots(split(a), split(b))


def wide(w_t):
    high = rounded(w_t)
    return jnp.concatenate([high, high, w_t - high], 0).T.astype(BF16)


def wide_rows(w):
    high, low = split(w)
    return jnp.concatenate([high, high, low], 1)


def tall(x):
    high, low = split(x)
    return jnp.concatenate([high, low, high], 0)


def tall_small(x):
    high = rounded(x)
    return jnp.concatenate([high, x - high, high], 0).astype(BF16)


def silu_pair(x):
    gate = 1.0 / (1.0 + jnp.exp(-x))
    return x * gate, gate * (1.0 + x * (1.0 - gate))


def lanes_from(x, index):
    return jnp.take_along_axis(x, index, axis=1, mode="promise_in_bounds")


def column_of(row, width=128):
    return jnp.broadcast_to(row, (width, row.shape[1])).T


def roll_up(x, amount):
    return pltpu.roll(x, 128 - amount, 1)


def pack_kernel(*refs):
    sources, out, copies, sems = refs[:6], refs[6], refs[7:13], refs[13]
    moves = [pltpu.make_async_copy(s, d, sems.at[i]) for i, (s, d) in enumerate(zip(sources, copies))]
    for move in moves:
        move.start()
    for move in moves:
        move.wait()
    pos, species, senders, counts, owners, send_list = copies
    for i in range(3):
        out[i : i + 1, :] = pos[i]
        out[4 + i : 5 + i, :] = senders[i].astype(F32)
        out[8 + i : 9 + i, :] = owners[i].astype(F32)
    out[3:4, :] = species[...].astype(F32)
    out[7:8, :] = counts[...].astype(F32)
    picked = jnp.broadcast_to(send_list[...].astype(F32), (128, 64)).T
    lane = lax.broadcasted_iota(jnp.int32, (64, 128), 1).astype(F32)
    row = lax.broadcasted_iota(jnp.int32, (64, 128), 0).astype(F32)
    slot = jnp.max(jnp.where(picked == lane, row, -1.0), axis=0, keepdims=True)
    out[11:16, :] = jnp.broadcast_to(slot, (5, 128))


def main_kernel(
    odd,
    mid,
    near_a,
    near_b,
    atom_table_hbm,
    edge_table_hbm,
    embedding_hbm,
    in_one_hbm,
    mid_one_hbm,
    out_one_hbm,
    mixing_hbm,
    square_mix_hbm,
    readout_one_hbm,
    in_two_hbm,
    mid_two_hbm,
    out_two_hbm,
    mix_two_hbm,
    read_hidden_hbm,
    read_out_hbm,
    forces,
    energies,
    hot0,
    hot1,
    hot2,
    emb_tab,
    spec_row,
    emb_edge,
    carried,
    shape_row,
    moments,
    squares,
    scalar_feat,
    feats,
    gathered_ref,
    proj,
    mix_split,
    mix_back,
    w_two,
    queue,
    square_grad,
    shape_grad,
    radial_grad,
    slopes,
    stack,
    left_ref,
    grad_ref,
    raw_ref,
    atom_table,
    edge_table,
    embedding,
    in_one,
    mid_one,
    out_one,
    mixing,
    square_mix,
    readout_one,
    in_two,
    mid_two,
    out_two,
    mix_two,
    read_hidden,
    read_out,
    sems,
):
    moves = [
        pltpu.make_async_copy(source, target, sems.at[i])
        for i, (source, target) in enumerate(
            (
                (atom_table_hbm, atom_table),
                (edge_table_hbm, edge_table),
                (embedding_hbm, embedding),
                (in_one_hbm, in_one),
                (mid_one_hbm, mid_one),
                (out_one_hbm, out_one),
                (mixing_hbm, mixing),
                (square_mix_hbm, square_mix),
                (readout_one_hbm, readout_one),
                (in_two_hbm, in_two),
                (mid_two_hbm, mid_two),
                (out_two_hbm, out_two),
                (mix_two_hbm, mix_two),
                (read_hidden_hbm, read_hidden),
                (read_out_hbm, read_out),
            )
        )
    ]
    for move in moves:
        move.start()
    moves[0].wait()
    moves[1].wait()
    lane256 = lax.broadcasted_iota(jnp.int32, (16, 256), 1) % 128
    from_a = (lane256 // 64) == odd[0]
    x_outer = jnp.where(from_a, near_a[...], near_b[...])
    own = mid[:, 0:128]
    sources = (x_outer[:, 0:128], mid[:, 128:256], x_outer[:, 128:256])
    row16 = lax.broadcasted_iota(jnp.int32, (16, 128), 0)
    atom_tiles = [own]
    key_b = []
    for t in range(4):
        cut = slice(128 * t, 128 * t + 128)
        if t:
            index = jnp.broadcast_to(atom_table[0:1, cut], (16, 128))
            which = jnp.broadcast_to(atom_table[1:2, cut], (16, 128))
            picked = [lanes_from(s, index) for s in sources]
            tile = jnp.where(which == 0, picked[0], jnp.where(which == 1, picked[1], picked[2]))
            block_x = jnp.broadcast_to(atom_table[2:3, cut].astype(F32), (16, 128))
            block_y = jnp.broadcast_to(atom_table[3:4, cut].astype(F32), (16, 128))
            shift = jnp.where(row16 == 0, block_x, jnp.where(row16 == 1, block_y, 0.0))
            atom_tiles.append(tile + shift * (SPACING * SIDE))
        slot = atom_tiles[t][11:12, :]
        code = atom_table[4:5, cut].astype(F32)
        key_b.append(jnp.where(slot < 0.0, -1.0, code * 192.0 + 128.0 + slot))
    lane16 = lax.broadcasted_iota(jnp.int32, (16, 128), 1)
    pack_two = lanes_from(atom_tiles[2], lane16 % 32)
    pack_three = lanes_from(atom_tiles[3], lane16 % 8)
    t0, t1, t2, t3 = atom_tiles
    receivers = jnp.concatenate([t0] * 3 + [t1] * 3 + [pack_two] + [t2] * 3 + [pack_three], 1)

    slot_row = edge_table[1:2, :]
    sent = jnp.where(
        slot_row == 0,
        receivers[4:5],
        jnp.where(slot_row == 1, receivers[5:6], receivers[6:7]),
    ).astype(jnp.int32)
    owned = jnp.where(
        slot_row == 0,
        receivers[8:9],
        jnp.where(slot_row == 1, receivers[9:10], receivers[10:11]),
    )
    live = (slot_row < receivers[7:8].astype(jnp.int32)).astype(F32)
    ghost = sent - 128
    block = lax.shift_right_arithmetic(ghost, 6)
    block = block + (block >= 4).astype(jnp.int32)
    code_row = edge_table[0:1, :]
    key = jnp.where(
        sent < 128,
        code_row * 192 + sent,
        (code_row + block - 4) * 192 + 128 + (ghost & 63),
    ).astype(F32)
    for c in range(4):
        cut = slice(128 * c, 128 * c + 128)
        plain = column_of(atom_table[5:6, cut].astype(F32))
        listed = column_of(key_b[c])
        for e in range(TILES):
            if (e < 3 and c > 1) or (e > 6 and c == 0):
                continue
            if e == 6 and c == 0:
                hot1[cut, 384:512] = jnp.zeros((128, 128), BF16)
                continue
            few = c == 3 and e < 7
            wanted = key[:, 128 * e : 128 * e + 128]
            rows = 16 if few else 128
            if c == 0 or e < 3:
                found = (plain if c == 0 and e < 3 else listed) == wanted
            else:
                found = (plain[0:rows] == wanted) | (listed[0:rows] == wanted)
            hit = jnp.where(found, 1.0, 0.0).astype(BF16)
            if few:
                hit = jnp.concatenate([hit, jnp.zeros((112, 128), BF16)], 0)
            if e < 3:
                hot0[cut, 128 * e : 128 * e + 128] = hit
            elif e < 7:
                hot1[cut, 128 * (e - 3) : 128 * (e - 3) + 128] = hit
            else:
                hot2[128 * c - 128 : 128 * c, 128 * (e - 7) : 128 * (e - 7) + 128] = hit

    raw = jnp.concatenate([t[0:8] for t in atom_tiles], 1)
    first = rounded(raw)
    second = rounded(raw - first)
    third = rounded(raw - first - second)
    terms = jnp.concatenate([first, second, third, third], 0).astype(BF16)
    found = jnp.concatenate(
        [mm(terms[:, 0:256], hot0[...]), mm(terms, hot1[...]), mm(terms[:, 128:512], hot2[...])], 1
    )
    found = found[0:8] + found[8:16] + found[16:24]
    away = [found[i : i + 1] - receivers[i : i + 1] for i in range(3)]
    spec_row[0:1, :] = found[3:4]
    spec_row[1:2, :] = live * (1.0 / 3.0)

    radius_sq = away[0] * away[0] + away[1] * away[1] + away[2] * away[2] + SOFTEN
    radius = jnp.sqrt(radius_sq)
    inverse = 1.0 / radius
    ux, uy, uz = [a * inverse for a in away]
    scaled = jnp.minimum(radius / CUTOFF, 1.0)
    s2 = scaled * scaled
    s3 = s2 * scaled
    s6 = s3 * s3
    envelope = 1.0 - 28.0 * s6 + 48.0 * s6 * scaled - 21.0 * s6 * s2
    slope = jnp.where(radius < CUTOFF, 1.0 / CUTOFF, 0.0)
    gap = 1.0 - scaled
    envelope_slope = -168.0 * s3 * s2 * gap * gap * slope
    order = (lax.broadcasted_iota(jnp.int32, (8, EDGES), 0) + 1).astype(F32)
    phase = order * (math.pi * scaled)
    factor = math.sqrt(2.0 / CUTOFF)
    sines = factor * jnp.sin(phase)
    basis = sines * (envelope * inverse)
    near = slice(0, EDGES_BACK)
    cosines = factor * jnp.cos(phase[:, near])
    basis_slope = (
        order[:, near] * cosines * (math.pi * slope * envelope * inverse)[:, near]
        + sines[:, near] * ((envelope_slope - envelope * inverse) * inverse)[:, near]
    )
    r3, r5, r15 = math.sqrt(3.0), math.sqrt(5.0), math.sqrt(15.0)
    shape_row[0:9, :] = jnp.concatenate(
        [
            jnp.ones_like(ux),
            r3 * ux,
            r3 * uy,
            r3 * uz,
            r15 * ux * uy,
            r15 * uy * uz,
            (0.5 * r5) * (2.0 * uz * uz - ux * ux - uy * uy),
            r15 * ux * uz,
            (0.5 * r15) * (ux * ux - uy * uy),
        ],
        0,
    )
    pair = owned * live * STRENGTH * jnp.exp(-radius)
    pair_slope = (pair * (envelope_slope - envelope))[:, near]
    pair = pair * envelope
    pair_own = pair[:, 0:128] + pair[:, 128:256] + pair[:, 256:384]

    for move in moves[2:]:
        move.wait()
    for z in range(5):
        emb_tab[z] = column_of(embedding[z : z + 1, :])

    def element(code):
        value = emb_tab[0]
        for z in range(1, 5):
            value = jnp.where(code == float(z), emb_tab[z], value)
        return value

    def embed_edges(e, carry):
        at = pl.ds(pl.multiple_of(e * 128, 128), 128)
        emb_edge[:, at] = element(spec_row[0:1, at]) * spec_row[1:2, at]
        return carry

    lax.fori_loop(0, TILES, embed_edges, 0)

    def out_parts(weight):
        return [wide(weight[:, 128 * g : 128 * g + 128]) for g in range(3)]

    net_one = (wide(in_one[...]), wide(mid_one[...].T), out_parts(out_one))
    net_two = (wide(in_two[...]), wide(mid_two[...].T), out_parts(out_two))
    chunks = [slice(i, min(i + 256, EDGES)) for i in range(0, EDGES, 256)]
    chunks_two = [slice(i, min(i + 256, EDGES_TWO)) for i in range(0, EDGES_TWO, 256)]
    jobs = [(net_one, c, 0) for c in chunks] + [(net_two, c, 1) for c in chunks_two]

    def layer(weight, source, chunk, slot, keep):
        value, slope_here = silu_pair(mm(weight, source))
        if chunk.start < EDGES_BACK:
            slopes[keep, :, chunk] = slope_here
        stack[slot, :, chunk] = tall(value)

    for net, chunk, slot in jobs:
        layer(net[0], tall_small(basis[:, chunk]), chunk, slot, 2 * slot)
    for net, chunk, slot in jobs:
        layer(net[1], stack[slot, :, chunk], chunk, slot, 2 * slot + 1)
    for net, chunk, slot in jobs:
        for g in range(3):
            weight = mm(net[2][g], stack[slot, :, chunk])
            if slot:
                w_two[g, :, chunk] = weight
            else:
                carried[g, :, chunk] = weight * emb_edge[:, chunk]

    for g in range(3):
        mix_split[g] = wide_rows(mixing[g])
        mix_back[g] = wide_rows(mixing[g].T)

    def degree(m):
        return int(m > 0) + int(m > 3)

    def moment(m, half):
        g = degree(m)
        y = shape_row[m : m + 1, :]

        def part(e):
            at = slice(128 * e, 128 * e + 128)
            return carried[g, :, at] * y[:, at] if m else carried[g, :, at]

        if half == 0:
            one = part(0) + part(1) + part(2)
            two = part(3) + part(4) + part(5)
        else:
            one = part(7) + part(8) + part(9)
            two = part(10)
            two = two + roll_up(two, 8) + roll_up(two, 16)
        at = slice(256 * half, 256 * half + 256)
        value = jnp.concatenate([one, two], 1)
        moments[m, :, at] = value
        if m:
            squares[:, at] += value * value
        else:
            squares[:, at] = value * value
        mixed = mm(mix_split[g], tall(value))
        if m:
            high, low = split(mixed)
            feats[m, 0:128, at] = high
            feats[m, 128:256, at] = low
        else:
            scalar_feat[:, at] = mixed

    def gather(m, at, first):
        g = degree(m)
        y = shape_row[m : m + 1, :]
        if at.start < 384:
            part = mm(feats[m, :, 0:256], hot0[:, at])
        else:
            part = mm(feats[m], hot1[:, at.start - 384 : at.stop - 384])
        part = part[0:128] + part[128:256]
        gathered_ref[m, :, at] = part
        if m:
            part = part * y[:, at]
        if first:
            proj[g, :, at] = part
        else:
            proj[g, :, at] += part

    spans = (slice(0, 256), slice(256, 384), slice(384, 640), slice(640, 896))
    for m in range(9):
        for half in range(2):
            moment(m, half)
            if m > 1:
                for at in spans[2 * half : 2 * half + 2]:
                    gather(m - 1, at, m - 1 in (1, 4))
    for at in spans[0:2]:
        gather(8, at, False)
    element_rows = jnp.concatenate([t[3:4] for t in atom_tiles], 1)
    scalar = scalar_feat[...] + mm(wide_rows(square_mix[...]), tall(squares[...]))
    scalar = scalar + jnp.concatenate(
        [element(element_rows[:, 128 * t : 128 * t + 128]) for t in range(4)], 1
    )
    scalar_feat[...] = scalar
    high, low = split(scalar)
    feats[0, 0:128, :] = high
    feats[0, 128:256, :] = low
    for at in spans[2:4]:
        gather(8, at, False)
    for at in spans:
        gather(0, at, True)

    live_two = live[:, 0:EDGES_TWO] * (1.0 / 3.0)
    term = (w_two[0] * proj[0] + w_two[1] * proj[1] + w_two[2] * proj[2]) * live_two
    tail = term[:, 768:896]
    total = jnp.concatenate(
        [
            term[:, 0:128] + term[:, 128:256] + term[:, 256:384],
            term[:, 384:512] + term[:, 512:640] + term[:, 640:768],
            tail + roll_up(tail, 32) + roll_up(tail, 64),
        ],
        1,
    )
    refined = mm(wide_rows(mix_two[...]), tall(total)) + scalar_feat[:, 0:384]
    hidden = mm(wide_rows(read_hidden[...]), tall(refined))
    act, dact = silu_pair(hidden)
    out_column = jnp.broadcast_to(column_of(read_out[...])[:, 0:1], (16, 384))
    one_column = column_of(readout_one[...])
    energies[...] = (
        jnp.sum(act[:, 0:128] * out_column[:, 0:128], axis=0, keepdims=True)
        + jnp.sum(scalar_feat[:, 0:128] * one_column, axis=0, keepdims=True)
        + pair_own
    )

    refined_grad = mm(wide(read_hidden[...]), tall(dact * out_column))
    total_grad = mm(wide_rows(mix_two[...].T), tall(refined_grad))
    lane128 = lax.broadcasted_iota(jnp.int32, (128, 128), 1)
    tail = jnp.where(lane128 < 32, total_grad[:, 256:384], 0.0)
    tail = tail + pltpu.roll(tail, 32, 1) + pltpu.roll(tail, 64, 1)
    grad0, grad1 = total_grad[:, 0:128], total_grad[:, 128:256]
    term_grad = jnp.concatenate([grad0] * 3 + [grad1] * 3 + [tail], 1) * live_two
    for g in range(3):
        queue[g] = term_grad * w_two[g]
        proj[g, :, near] = term_grad[:, near] * proj[g, :, near]
    def spread_edges(m):
        g = degree(m)
        y = shape_row[m : m + 1, :]
        for row in range(0, 128, 16):
            rows = slice(row, row + 16)
            part = queue[g, rows, :]
            high, low = split(part * y[:, 0:EDGES_TWO] if m else part)
            left_ref[m % 3, rows, :] = high
            left_ref[m % 3, 128 + row : 144 + row, :] = low

    def scatter(m):
        grad = mm_nt(left_ref[m % 3, :, 0:384], hot0[...])
        grad = grad + mm_nt(left_ref[m % 3, :, 384:896], hot1[0:256, :])
        raw_ref[m % 3] = grad[0:128] + grad[128:256]

    def unmix(m):
        grad = raw_ref[m % 3]
        if m == 0:
            grad = grad + refined_grad[:, 0:256] + jnp.concatenate([one_column] * 2, 1)
            square_grad[...] = 2.0 * mm(wide_rows(square_mix[...].T), tall(grad))
        grad = mm(mix_back[degree(m)], tall(grad))
        grad_ref[m % 3] = grad + square_grad[...] * moments[m, :, 0:256]

    def edge_parts(m, start, total):
        g = degree(m)
        y = shape_row[m : m + 1, :]
        for row in range(start, start + 64, 8):
            rows = slice(row, row + 8)
            here = grad_ref[m % 3, rows, :]
            here = jnp.concatenate([here[:, 0:128]] * 3 + [here[:, 128:256]] * 3, 1)
            both = queue[g, rows, near] * gathered_ref[m, rows, near]
            both = both + here * carried[g, rows, near]
            total = both if total is None else total + both
            here = here * y[:, near] if m else here
            if m in (0, 1, 4):
                radial_grad[g, rows, :] = here
            else:
                radial_grad[g, rows, :] += here
        return total

    for step in range(11):
        total = None
        if step < 9:
            spread_edges(step)
            scatter(step)
        if step > 1:
            total = edge_parts(step - 2, 0, None)
        if 0 < step < 10:
            unmix(step - 1)
        if step > 1:
            total = edge_parts(step - 2, 64, total)
            shape_grad[step - 2 : step - 1, :] = jnp.sum(total, axis=0, keepdims=True)

    back_one = (jnp.concatenate(split(out_one[...]), 0), wide(mid_one[...]), wide(in_one[...].T))
    back_two = (jnp.concatenate(split(out_two[...]), 0), wide(mid_two[...]), wide(in_two[...].T))

    def network_back(weights, grads, chunk, slot):
        high, low = split(jnp.concatenate(grads, 0))
        top_grad = mm(weights[0], high)
        top_grad = top_grad[0:64] + top_grad[64:128] + mm(weights[0][0:64], low)
        hid_grad = mm(weights[1], tall(top_grad * slopes[slot + 1, :, chunk]))
        return mm(weights[2], tall(hid_grad * slopes[slot, :, chunk]))

    parts = []
    for start in range(0, EDGES_BACK, 256):
        chunk = slice(start, start + 256)
        ones = [radial_grad[g, :, chunk] * emb_edge[:, chunk] for g in range(3)]
        twos = [proj[g, :, chunk] for g in range(3)]
        parts.append(
            network_back(back_one, ones, chunk, 0) + network_back(back_two, twos, chunk, 2)
        )
    basis_grad = jnp.concatenate(parts, 1)

    ux, uy, uz, inverse = ux[:, near], uy[:, near], uz[:, near], inverse[:, near]
    ym = [shape_grad[m : m + 1, :] for m in range(9)]
    gx = r3 * ym[1] + r15 * (uy * ym[4] + uz * ym[7] + ux * ym[8]) - r5 * ux * ym[6]
    gy = r3 * ym[2] + r15 * (ux * ym[4] + uz * ym[5] - uy * ym[8]) - r5 * uy * ym[6]
    gz = r3 * ym[3] + r15 * (uy * ym[5] + ux * ym[7]) + 2.0 * r5 * uz * ym[6]
    along = jnp.sum(basis_grad * basis_slope, axis=0, keepdims=True) + pair_slope
    along = along - (gx * ux + gy * uy + gz * uz) * inverse
    keep = edge_table[2:3, near].astype(F32)
    edge_grad = jnp.concatenate(
        [(gx * inverse + along * ux) * keep, (gy * inverse + along * uy) * keep,
         (gz * inverse + along * uz) * keep, jnp.zeros((5, EDGES_BACK), F32)],
        0,
    )
    high = rounded(edge_grad)
    left = jnp.concatenate([high, edge_grad - high], 0).astype(BF16)
    pulled = mm_nt(left[:, 0:384], hot0[0:128, :]) + mm_nt(left[:, 384:768], hot1[0:128, 0:384])
    pulled = pulled[0:8] + pulled[8:16]
    mine = edge_grad[:, 0:128] + edge_grad[:, 128:256] + edge_grad[:, 256:384]
    total = mine - pulled
    for i in range(3):
        forces[i] = total[i : i + 1]


def swap(value, axis, odd):
    count = lax.axis_size(axis)
    pairs = [(i, (((i - odd) ^ 1) + odd) % count) for i in range(count)]
    return lax.ppermute(value, axis, pairs)


def local(
    positions,
    species,
    senders,
    counts,
    owners,
    send_list,
    embedding,
    radial_in_one,
    radial_mid_one,
    radial_out_one,
    mixing,
    square_mix,
    readout_one,
    radial_in_two,
    radial_mid_two,
    radial_out_two,
    mix_two,
    read_hidden,
    read_out,
):
    packed = pl.pallas_call(
        pack_kernel,
        out_shape=jax.ShapeDtypeStruct((16, 128), F32),
        in_specs=[pl.BlockSpec(memory_space=pltpu.HBM)] * 6,
        out_specs=pl.BlockSpec(memory_space=pltpu.VMEM),
        scratch_shapes=[
            pltpu.VMEM((3, 1, 128), F32),
            pltpu.VMEM((1, 128), jnp.int32),
            pltpu.VMEM((3, 1, 128), jnp.int32),
            pltpu.VMEM((1, 128), jnp.int32),
            pltpu.VMEM((3, 1, 128), jnp.int32),
            pltpu.VMEM((1, 64), jnp.int32),
            pltpu.SemaphoreType.DMA((6,)),
        ],
        interpret=INTERPRET,
    )(
        positions.reshape(3, 1, 128),
        species[0],
        senders.reshape(3, 1, 128),
        counts[0],
        owners.reshape(3, 1, 128),
        send_list[0],
    )
    near_a, near_b = swap(packed, "gy", 0), swap(packed, "gy", 1)
    odd_y = lax.axis_index("gy") % 2
    lane = lax.broadcasted_iota(jnp.int32, (16, 128), 1)
    outer = jnp.where(lane // 8 % 2 == odd_y, near_a, near_b)
    mid = jnp.concatenate([packed, outer], 1)
    near_a, near_b = swap(mid, "gx", 0), swap(mid, "gx", 1)
    odd_x = (lax.axis_index("gx") % 2).astype(jnp.int32).reshape(1)
    held = (
        jnp.asarray(ATOM_TABLE),
        jnp.asarray(EDGE_TABLE),
        embedding.T,
        radial_in_one.T,
        radial_mid_one,
        radial_out_one.T,
        mixing,
        square_mix,
        readout_one.reshape(1, -1),
        radial_in_two.T,
        radial_mid_two,
        radial_out_two.T,
        mix_two,
        read_hidden,
        read_out.reshape(1, -1),
    )
    vmem = pl.BlockSpec(memory_space=pltpu.VMEM)
    forces, energies = pl.pallas_call(
        main_kernel,
        out_shape=(
            jax.ShapeDtypeStruct((3, 1, 128), F32),
            jax.ShapeDtypeStruct((1, 128), F32),
        ),
        in_specs=[pl.BlockSpec(memory_space=pltpu.SMEM)]
        + [vmem] * 3
        + [pl.BlockSpec(memory_space=pltpu.HBM)] * len(held),
        out_specs=(vmem, vmem),
        scratch_shapes=[
            pltpu.VMEM((256, 384), BF16),
            pltpu.VMEM((512, 512), BF16),
            pltpu.VMEM((384, 512), BF16),
            pltpu.VMEM((5, 128, 128), F32),
            pltpu.VMEM((8, EDGES), F32),
            pltpu.VMEM((128, EDGES), F32),
            pltpu.VMEM((3, 128, EDGES), F32),
            pltpu.VMEM((16, EDGES), F32),
            pltpu.VMEM((9, 128, 512), F32),
            pltpu.VMEM((128, 512), F32),
            pltpu.VMEM((128, 512), F32),
            pltpu.VMEM((9, 256, 512), BF16),
            pltpu.VMEM((9, 128, EDGES_TWO), F32),
            pltpu.VMEM((3, 128, EDGES_TWO), F32),
            pltpu.VMEM((3, 128, 384), BF16),
            pltpu.VMEM((3, 128, 384), BF16),
            pltpu.VMEM((3, 128, EDGES_TWO), F32),
            pltpu.VMEM((3, 128, EDGES_TWO), F32),
            pltpu.VMEM((128, 256), F32),
            pltpu.VMEM((16, EDGES_BACK), F32),
            pltpu.VMEM((3, 128, EDGES_BACK), F32),
            pltpu.VMEM((4, 64, EDGES_BACK), F32),
            pltpu.VMEM((2, 192, EDGES), BF16),
            pltpu.VMEM((3, 256, EDGES_TWO), BF16),
            pltpu.VMEM((3, 128, 256), F32),
            pltpu.VMEM((3, 128, 256), F32),
        ]
        + [pltpu.VMEM(h.shape, h.dtype) for h in held]
        + [pltpu.SemaphoreType.DMA((len(held),))],
        interpret=INTERPRET,
    )(odd_x, mid, near_a, near_b, *held)
    return forces.reshape(1, 1, 3, 128), energies[None]


def solution(mesh):
    split_four = P("gx", "gy", None, None)
    split_three = P("gx", "gy", None)
    placed = (split_four, split_three, split_four, split_three, split_four, split_three)
    return jax.shard_map(
        local,
        mesh=mesh,
        in_specs=placed + (P(),) * 13,
        out_specs=(split_four, split_three),
        check_vma=False,
    )
```

```python
import math

import jax
import jax.numpy as jnp
import numpy as np
from jax import lax
from jax.experimental import pallas as pl
from jax.experimental.pallas import tpu as pltpu
from jax.sharding import PartitionSpec as P

SIDE = 8
SPACING = 1.75
CUTOFF = 5.0
SOFTEN = 0.25
STRENGTH = 2.0
F32 = jnp.float32
BF16 = jnp.bfloat16
INTERPRET = False

TILES = 11
EDGES = TILES * 128
EDGES_TWO = 7 * 128
EDGES_BACK = 6 * 128


def tables():
    lane = np.arange(128)
    site_x, site_y = lane // 16, lane // 2 % 8

    def outer(site):
        low = site >= 4
        return np.where(low, -1, 1), np.where(low, 8 - site, site + 1)

    block_x, ring_x = outer(site_x)
    block_y, ring_y = outer(site_y)
    none = np.zeros(128, np.int64)
    rings = np.concatenate([ring_x, ring_y, np.maximum(ring_x, ring_y)])
    blocks_x = np.concatenate([block_x, none, block_x])
    blocks_y = np.concatenate([none, block_y, block_y])
    source = np.concatenate([none, none + 1, none + 2])
    order = np.argsort(rings, kind="stable")
    atoms = np.zeros((8, 512), np.int64)
    atoms[0] = np.concatenate([lane, np.tile(lane, 3)[order]])
    atoms[1] = np.concatenate([none, source[order]])
    atoms[2] = np.concatenate([none, blocks_x[order]])
    atoms[3] = np.concatenate([none, blocks_y[order]])
    code = 3 * (atoms[2] + 1) + atoms[3] + 1
    atoms[4] = code
    atoms[5] = code * 192 + atoms[0]
    edges = np.zeros((8, EDGES), np.int64)
    tile_code = code.reshape(4, 128)
    edges[0] = np.concatenate(
        [tile_code[0]] * 3
        + [tile_code[1]] * 3
        + [tile_code[2][lane % 32]]
        + [tile_code[2]] * 3
        + [tile_code[3][lane % 8]]
    )
    two = np.where(lane < 96, lane // 32, 9)
    three = np.where(lane < 24, lane // 8, 9)
    slots = [none, none + 1, none + 2]
    edges[1] = np.concatenate(slots + slots + [two] + slots + [three])
    near = (lane < 72).astype(np.int64)
    edges[2] = np.concatenate([none + 1] * 3 + [near] * 3 + [none] * 5)
    return atoms.astype(np.int32), edges.astype(np.int32)


ATOM_TABLE, EDGE_TABLE = tables()


def rounded(x):
    return x.astype(BF16).astype(F32)


def split(x):
    high = x.astype(BF16)
    return high, (x - high.astype(F32)).astype(BF16)


def mm(a, b):
    return lax.dot_general(a, b, (((1,), (0,)), ((), ())), preferred_element_type=F32)


def mm_nt(a, b):
    return lax.dot_general(a, b, (((1,), (1,)), ((), ())), preferred_element_type=F32)


def dots(a, b):
    return mm(a[0], b[0]) + mm(a[0], b[1]) + mm(a[1], b[0])


def dot3(a, b):
    return dots(split(a), split(b))


def wide(w_t):
    high = rounded(w_t)
    return jnp.concatenate([high, high, w_t - high], 0).T.astype(BF16)


def wide_rows(w):
    high, low = split(w)
    return jnp.concatenate([high, high, low], 1)


def tall(x):
    high, low = split(x)
    return jnp.concatenate([high, low, high], 0)


def tall_small(x):
    high = rounded(x)
    return jnp.concatenate([high, x - high, high], 0).astype(BF16)


def silu_pair(x):
    gate = 1.0 / (1.0 + jnp.exp(-x))
    return x * gate, gate * (1.0 + x * (1.0 - gate))


def lanes_from(x, index):
    return jnp.take_along_axis(x, index, axis=1, mode="promise_in_bounds")


def column_of(row, width=128):
    return jnp.broadcast_to(row, (width, row.shape[1])).T


def roll_up(x, amount):
    return pltpu.roll(x, 128 - amount, 1)


def pack_kernel(*refs):
    sources, out, copies, sems = refs[:6], refs[6], refs[7:13], refs[13]
    moves = [pltpu.make_async_copy(s, d, sems.at[i]) for i, (s, d) in enumerate(zip(sources, copies))]
    for move in moves:
        move.start()
    for move in moves:
        move.wait()
    pos, species, senders, counts, owners, send_list = copies
    for i in range(3):
        out[i : i + 1, :] = pos[i]
        out[4 + i : 5 + i, :] = senders[i].astype(F32)
        out[8 + i : 9 + i, :] = owners[i].astype(F32)
    out[3:4, :] = species[...].astype(F32)
    out[7:8, :] = counts[...].astype(F32)
    picked = jnp.broadcast_to(send_list[...].astype(F32), (128, 64)).T
    lane = lax.broadcasted_iota(jnp.int32, (64, 128), 1).astype(F32)
    row = lax.broadcasted_iota(jnp.int32, (64, 128), 0).astype(F32)
    slot = jnp.max(jnp.where(picked == lane, row, -1.0), axis=0, keepdims=True)
    out[11:16, :] = jnp.broadcast_to(slot, (5, 128))


def main_kernel(
    odd,
    mid,
    near_a,
    near_b,
    atom_table_hbm,
    edge_table_hbm,
    embedding_hbm,
    in_one_hbm,
    mid_one_hbm,
    out_one_hbm,
    mixing_hbm,
    square_mix_hbm,
    readout_one_hbm,
    in_two_hbm,
    mid_two_hbm,
    out_two_hbm,
    mix_two_hbm,
    read_hidden_hbm,
    read_out_hbm,
    forces,
    energies,
    hot0,
    hot1,
    hot2,
    emb_tab,
    spec_row,
    emb_edge,
    carried,
    shape_row,
    moments,
    squares,
    scalar_feat,
    feats,
    gathered_ref,
    proj,
    mix_split,
    mix_back,
    w_two,
    queue,
    square_grad,
    shape_grad,
    radial_grad,
    slopes,
    stack,
    left_ref,
    grad_ref,
    raw_ref,
    square_back,
    atom_table,
    edge_table,
    embedding,
    in_one,
    mid_one,
    out_one,
    mixing,
    square_mix,
    readout_one,
    in_two,
    mid_two,
    out_two,
    mix_two,
    read_hidden,
    read_out,
    sems,
):
    moves = [
        pltpu.make_async_copy(source, target, sems.at[i])
        for i, (source, target) in enumerate(
            (
                (atom_table_hbm, atom_table),
                (edge_table_hbm, edge_table),
                (embedding_hbm, embedding),
                (in_one_hbm, in_one),
                (mid_one_hbm, mid_one),
                (out_one_hbm, out_one),
                (mixing_hbm, mixing),
                (square_mix_hbm, square_mix),
                (readout_one_hbm, readout_one),
                (in_two_hbm, in_two),
                (mid_two_hbm, mid_two),
                (out_two_hbm, out_two),
                (mix_two_hbm, mix_two),
                (read_hidden_hbm, read_hidden),
                (read_out_hbm, read_out),
            )
        )
    ]
    for move in moves:
        move.start()
    moves[0].wait()
    moves[1].wait()
    lane256 = lax.broadcasted_iota(jnp.int32, (16, 256), 1) % 128
    from_a = (lane256 // 64) == odd[0]
    x_outer = jnp.where(from_a, near_a[...], near_b[...])
    own = mid[:, 0:128]
    sources = (x_outer[:, 0:128], mid[:, 128:256], x_outer[:, 128:256])
    row16 = lax.broadcasted_iota(jnp.int32, (16, 128), 0)
    atom_tiles = [own]
    key_b = []
    for t in range(4):
        cut = slice(128 * t, 128 * t + 128)
        if t:
            index = jnp.broadcast_to(atom_table[0:1, cut], (16, 128))
            which = jnp.broadcast_to(atom_table[1:2, cut], (16, 128))
            picked = [lanes_from(s, index) for s in sources]
            tile = jnp.where(which == 0, picked[0], jnp.where(which == 1, picked[1], picked[2]))
            block_x = jnp.broadcast_to(atom_table[2:3, cut].astype(F32), (16, 128))
            block_y = jnp.broadcast_to(atom_table[3:4, cut].astype(F32), (16, 128))
            shift = jnp.where(row16 == 0, block_x, jnp.where(row16 == 1, block_y, 0.0))
            atom_tiles.append(tile + shift * (SPACING * SIDE))
        slot = atom_tiles[t][11:12, :]
        code = atom_table[4:5, cut].astype(F32)
        key_b.append(jnp.where(slot < 0.0, -1.0, code * 192.0 + 128.0 + slot))
    lane16 = lax.broadcasted_iota(jnp.int32, (16, 128), 1)
    pack_two = lanes_from(atom_tiles[2], lane16 % 32)
    pack_three = lanes_from(atom_tiles[3], lane16 % 8)
    t0, t1, t2, t3 = atom_tiles
    receivers = jnp.concatenate([t0] * 3 + [t1] * 3 + [pack_two] + [t2] * 3 + [pack_three], 1)

    slot_row = edge_table[1:2, :]
    sent = jnp.where(
        slot_row == 0,
        receivers[4:5],
        jnp.where(slot_row == 1, receivers[5:6], receivers[6:7]),
    ).astype(jnp.int32)
    owned = jnp.where(
        slot_row == 0,
        receivers[8:9],
        jnp.where(slot_row == 1, receivers[9:10], receivers[10:11]),
    )
    live = (slot_row < receivers[7:8].astype(jnp.int32)).astype(F32)
    ghost = sent - 128
    block = lax.shift_right_arithmetic(ghost, 6)
    block = block + (block >= 4).astype(jnp.int32)
    code_row = edge_table[0:1, :]
    key = jnp.where(
        sent < 128,
        code_row * 192 + sent,
        (code_row + block - 4) * 192 + 128 + (ghost & 63),
    ).astype(F32)
    for c in range(4):
        cut = slice(128 * c, 128 * c + 128)
        plain = column_of(atom_table[5:6, cut].astype(F32))
        listed = column_of(key_b[c])
        for e in range(TILES):
            if (e < 3 and c > 1) or (e > 6 and c == 0):
                continue
            if e == 6 and c == 0:
                hot1[cut, 384:512] = jnp.zeros((128, 128), BF16)
                continue
            few = c == 3 and e < 7
            wanted = key[:, 128 * e : 128 * e + 128]
            rows = 16 if few else 128
            if c == 0 or e < 3:
                found = (plain if c == 0 and e < 3 else listed) == wanted
            else:
                found = (plain[0:rows] == wanted) | (listed[0:rows] == wanted)
            hit = jnp.where(found, 1.0, 0.0).astype(BF16)
            if few:
                hit = jnp.concatenate([hit, jnp.zeros((112, 128), BF16)], 0)
            if e < 3:
                hot0[cut, 128 * e : 128 * e + 128] = hit
            elif e < 7:
                hot1[cut, 128 * (e - 3) : 128 * (e - 3) + 128] = hit
            else:
                hot2[128 * c - 128 : 128 * c, 128 * (e - 7) : 128 * (e - 7) + 128] = hit

    raw = jnp.concatenate([t[0:8] for t in atom_tiles], 1)
    first = rounded(raw)
    second = rounded(raw - first)
    third = rounded(raw - first - second)
    terms = jnp.concatenate([first, second, third, third], 0).astype(BF16)
    found = jnp.concatenate(
        [mm(terms[:, 0:256], hot0[...]), mm(terms, hot1[...]), mm(terms[:, 128:512], hot2[...])], 1
    )
    found = found[0:8] + found[8:16] + found[16:24]
    away = [found[i : i + 1] - receivers[i : i + 1] for i in range(3)]
    spec_row[0:1, :] = found[3:4]
    spec_row[1:2, :] = live * (1.0 / 3.0)

    radius_sq = away[0] * away[0] + away[1] * away[1] + away[2] * away[2] + SOFTEN
    radius = jnp.sqrt(radius_sq)
    inverse = 1.0 / radius
    ux, uy, uz = [a * inverse for a in away]
    scaled = jnp.minimum(radius / CUTOFF, 1.0)
    s2 = scaled * scaled
    s3 = s2 * scaled
    s6 = s3 * s3
    envelope = 1.0 - 28.0 * s6 + 48.0 * s6 * scaled - 21.0 * s6 * s2
    slope = jnp.where(radius < CUTOFF, 1.0 / CUTOFF, 0.0)
    gap = 1.0 - scaled
    envelope_slope = -168.0 * s3 * s2 * gap * gap * slope
    order = (lax.broadcasted_iota(jnp.int32, (8, EDGES), 0) + 1).astype(F32)
    phase = order * (math.pi * scaled)
    factor = math.sqrt(2.0 / CUTOFF)
    sines = factor * jnp.sin(phase)
    basis = sines * (envelope * inverse)
    near = slice(0, EDGES_BACK)
    cosines = factor * jnp.cos(phase[:, near])
    basis_slope = (
        order[:, near] * cosines * (math.pi * slope * envelope * inverse)[:, near]
        + sines[:, near] * ((envelope_slope - envelope * inverse) * inverse)[:, near]
    )
    r3, r5, r15 = math.sqrt(3.0), math.sqrt(5.0), math.sqrt(15.0)
    shape_row[0:9, :] = jnp.concatenate(
        [
            jnp.ones_like(ux),
            r3 * ux,
            r3 * uy,
            r3 * uz,
            r15 * ux * uy,
            r15 * uy * uz,
            (0.5 * r5) * (2.0 * uz * uz - ux * ux - uy * uy),
            r15 * ux * uz,
            (0.5 * r15) * (ux * ux - uy * uy),
        ],
        0,
    )
    pair = owned * live * STRENGTH * jnp.exp(-radius)
    pair_slope = (pair * (envelope_slope - envelope))[:, near]
    pair = pair * envelope
    pair_own = pair[:, 0:128] + pair[:, 128:256] + pair[:, 256:384]

    for move in moves[2:]:
        move.wait()
    for z in range(5):
        emb_tab[z] = column_of(embedding[z : z + 1, :])

    def element(code):
        value = emb_tab[0]
        for z in range(1, 5):
            value = jnp.where(code == float(z), emb_tab[z], value)
        return value

    def embed_edges(e, carry):
        at = pl.ds(pl.multiple_of(e * 128, 128), 128)
        emb_edge[:, at] = element(spec_row[0:1, at]) * spec_row[1:2, at]
        return carry

    lax.fori_loop(0, TILES, embed_edges, 0)

    def out_parts(weight):
        return [wide(weight[:, 128 * g : 128 * g + 128]) for g in range(3)]

    net_one = (wide(in_one[...]), wide(mid_one[...].T), out_parts(out_one))
    net_two = (wide(in_two[...]), wide(mid_two[...].T), out_parts(out_two))
    chunks = [slice(i, min(i + 256, EDGES)) for i in range(0, EDGES, 256)]
    chunks_two = [slice(i, min(i + 256, EDGES_TWO)) for i in range(0, EDGES_TWO, 256)]
    jobs = [(net_one, c, 0) for c in chunks] + [(net_two, c, 1) for c in chunks_two]

    def layer(weight, source, chunk, slot, keep):
        value, slope_here = silu_pair(mm(weight, source))
        if chunk.start < EDGES_BACK:
            slopes[keep, :, chunk] = slope_here
        stack[slot, :, chunk] = tall(value)

    for net, chunk, slot in jobs:
        layer(net[0], tall_small(basis[:, chunk]), chunk, slot, 2 * slot)
    for net, chunk, slot in jobs:
        layer(net[1], stack[slot, :, chunk], chunk, slot, 2 * slot + 1)
    for net, chunk, slot in jobs:
        for g in range(3):
            weight = mm(net[2][g], stack[slot, :, chunk])
            if slot:
                w_two[g, :, chunk] = weight
            else:
                carried[g, :, chunk] = weight * emb_edge[:, chunk]

    for g in range(3):
        mix_split[g] = wide_rows(mixing[g])

    def degree(m):
        return int(m > 0) + int(m > 3)

    def moment(m, half):
        g = degree(m)
        y = shape_row[m : m + 1, :]

        def part(e):
            at = slice(128 * e, 128 * e + 128)
            return carried[g, :, at] * y[:, at] if m else carried[g, :, at]

        if half == 0:
            one = part(0) + part(1) + part(2)
            two = part(3) + part(4) + part(5)
        else:
            one = part(7) + part(8) + part(9)
            two = part(10)
            two = two + roll_up(two, 8) + roll_up(two, 16)
        at = slice(256 * half, 256 * half + 256)
        value = jnp.concatenate([one, two], 1)
        moments[m, :, at] = value
        if m:
            squares[:, at] += value * value
        else:
            squares[:, at] = value * value
        mixed = mm(mix_split[g], tall(value))
        if m:
            high, low = split(mixed)
            feats[m, 0:128, at] = high
            feats[m, 128:256, at] = low
        else:
            scalar_feat[:, at] = mixed

    def gather(m, at, first):
        g = degree(m)
        y = shape_row[m : m + 1, :]
        if at.start < 384:
            part = mm(feats[m, :, 0:256], hot0[:, at])
        else:
            part = mm(feats[m], hot1[:, at.start - 384 : at.stop - 384])
        part = part[0:128] + part[128:256]
        gathered_ref[m, :, at] = part
        if m:
            part = part * y[:, at]
        if first:
            proj[g, :, at] = part
        else:
            proj[g, :, at] += part

    spans = (slice(0, 256), slice(256, 384), slice(384, 640), slice(640, 896))
    for m in range(9):
        for half in range(2):
            moment(m, half)
            if m > 1:
                for at in spans[2 * half : 2 * half + 2]:
                    gather(m - 1, at, m - 1 in (1, 4))
    for at in spans[0:2]:
        gather(8, at, False)
    element_rows = jnp.concatenate([t[3:4] for t in atom_tiles], 1)
    scalar = scalar_feat[...] + mm(wide_rows(square_mix[...]), tall(squares[...]))
    scalar = scalar + jnp.concatenate(
        [element(element_rows[:, 128 * t : 128 * t + 128]) for t in range(4)], 1
    )
    scalar_feat[...] = scalar
    high, low = split(scalar)
    feats[0, 0:128, :] = high
    feats[0, 128:256, :] = low
    for at in spans[2:4]:
        gather(8, at, False)
    for at in spans:
        gather(0, at, True)

    live_two = live[:, 0:EDGES_TWO] * (1.0 / 3.0)
    term = (w_two[0] * proj[0] + w_two[1] * proj[1] + w_two[2] * proj[2]) * live_two
    tail = term[:, 768:896]
    total = jnp.concatenate(
        [
            term[:, 0:128] + term[:, 128:256] + term[:, 256:384],
            term[:, 384:512] + term[:, 512:640] + term[:, 640:768],
            tail + roll_up(tail, 32) + roll_up(tail, 64),
        ],
        1,
    )
    refined = mm(wide_rows(mix_two[...]), tall(total)) + scalar_feat[:, 0:384]
    for g in range(3):
        mix_back[g] = wide_rows(mixing[g].T)
    hidden = mm(wide_rows(read_hidden[...]), tall(refined))
    square_back[...] = wide_rows(square_mix[...].T)
    act, dact = silu_pair(hidden)
    out_column = jnp.broadcast_to(column_of(read_out[...])[:, 0:1], (16, 384))
    one_column = column_of(readout_one[...])
    energies[...] = (
        jnp.sum(act[:, 0:128] * out_column[:, 0:128], axis=0, keepdims=True)
        + jnp.sum(scalar_feat[:, 0:128] * one_column, axis=0, keepdims=True)
        + pair_own
    )

    refined_grad = mm(wide(read_hidden[...]), tall(dact * out_column))
    total_grad = mm(wide_rows(mix_two[...].T), tall(refined_grad))
    lane128 = lax.broadcasted_iota(jnp.int32, (128, 128), 1)
    tail = jnp.where(lane128 < 32, total_grad[:, 256:384], 0.0)
    tail = tail + pltpu.roll(tail, 32, 1) + pltpu.roll(tail, 64, 1)
    grad0, grad1 = total_grad[:, 0:128], total_grad[:, 128:256]
    term_grad = jnp.concatenate([grad0] * 3 + [grad1] * 3 + [tail], 1) * live_two
    for g in range(3):
        queue[g] = term_grad * w_two[g]
        proj[g, :, near] = term_grad[:, near] * proj[g, :, near]
    def spread_edges(m):
        g = degree(m)
        y = shape_row[m : m + 1, :]
        for row in range(0, 128, 16):
            rows = slice(row, row + 16)
            part = queue[g, rows, :]
            high, low = split(part * y[:, 0:EDGES_TWO] if m else part)
            left_ref[m % 3, rows, :] = high
            left_ref[m % 3, 128 + row : 144 + row, :] = low

    def scatter(m):
        grad = mm_nt(left_ref[m % 3, :, 0:384], hot0[...])
        grad = grad + mm_nt(left_ref[m % 3, :, 384:896], hot1[0:256, :])
        raw_ref[m % 3] = grad[0:128] + grad[128:256]

    def unmix(m):
        grad = raw_ref[m % 3]
        if m == 0:
            grad = grad + refined_grad[:, 0:256] + jnp.concatenate([one_column] * 2, 1)
            square_grad[...] = 2.0 * mm(square_back[...], tall(grad))
        grad = mm(mix_back[degree(m)], tall(grad))
        grad_ref[m % 3] = grad + square_grad[...] * moments[m, :, 0:256]

    def edge_parts(m, start, total):
        g = degree(m)
        y = shape_row[m : m + 1, :]
        for row in range(start, start + 64, 8):
            rows = slice(row, row + 8)
            here = grad_ref[m % 3, rows, :]
            here = jnp.concatenate([here[:, 0:128]] * 3 + [here[:, 128:256]] * 3, 1)
            both = queue[g, rows, near] * gathered_ref[m, rows, near]
            both = both + here * carried[g, rows, near]
            total = both if total is None else total + both
            here = here * y[:, near] if m else here
            if m in (0, 1, 4):
                radial_grad[g, rows, :] = here
            else:
                radial_grad[g, rows, :] += here
        return total

    for step in range(11):
        total = None
        if step < 9:
            spread_edges(step)
            scatter(step)
        if step > 1:
            total = edge_parts(step - 2, 0, None)
        if 0 < step < 10:
            unmix(step - 1)
        if step > 1:
            total = edge_parts(step - 2, 64, total)
            shape_grad[step - 2 : step - 1, :] = jnp.sum(total, axis=0, keepdims=True)

    back_one = (jnp.concatenate(split(out_one[...]), 0), wide(mid_one[...]), wide(in_one[...].T))
    back_two = (jnp.concatenate(split(out_two[...]), 0), wide(mid_two[...]), wide(in_two[...].T))

    def out_back(weights, grads, chunk, slot):
        high, low = split(jnp.concatenate(grads, 0))
        value = mm(weights[0], high)
        value = value[0:64] + value[64:128] + mm(weights[0][0:64], low)
        stack[slot // 2, :, chunk] = tall(value * slopes[slot + 1, :, chunk])

    parts = [slice(start, start + 256) for start in range(0, EDGES_BACK, 256)]
    nets = ((back_one, 0), (back_two, 2))
    for chunk in parts:
        twos = [proj[g, :, chunk] for g in range(3)]
        out_back(back_two, twos, chunk, 2)
        ones = [radial_grad[g, :, chunk] * emb_edge[:, chunk] for g in range(3)]
        out_back(back_one, ones, chunk, 0)
    for chunk in parts:
        for weights, slot in nets:
            value = mm(weights[1], stack[slot // 2, :, chunk])
            stack[slot // 2, :, chunk] = tall(value * slopes[slot, :, chunk])
    basis_grad = jnp.concatenate(
        [
            mm(back_one[2], stack[0, :, chunk]) + mm(back_two[2], stack[1, :, chunk])
            for chunk in parts
        ],
        1,
    )

    ux, uy, uz, inverse = ux[:, near], uy[:, near], uz[:, near], inverse[:, near]
    ym = [shape_grad[m : m + 1, :] for m in range(9)]
    gx = r3 * ym[1] + r15 * (uy * ym[4] + uz * ym[7] + ux * ym[8]) - r5 * ux * ym[6]
    gy = r3 * ym[2] + r15 * (ux * ym[4] + uz * ym[5] - uy * ym[8]) - r5 * uy * ym[6]
    gz = r3 * ym[3] + r15 * (uy * ym[5] + ux * ym[7]) + 2.0 * r5 * uz * ym[6]
    along = jnp.sum(basis_grad * basis_slope, axis=0, keepdims=True) + pair_slope
    along = along - (gx * ux + gy * uy + gz * uz) * inverse
    keep = edge_table[2:3, near].astype(F32)
    edge_grad = jnp.concatenate(
        [(gx * inverse + along * ux) * keep, (gy * inverse + along * uy) * keep,
         (gz * inverse + along * uz) * keep, jnp.zeros((5, EDGES_BACK), F32)],
        0,
    )
    high = rounded(edge_grad)
    left = jnp.concatenate([high, edge_grad - high], 0).astype(BF16)
    pulled = mm_nt(left[:, 0:384], hot0[0:128, :]) + mm_nt(left[:, 384:768], hot1[0:128, 0:384])
    pulled = pulled[0:8] + pulled[8:16]
    mine = edge_grad[:, 0:128] + edge_grad[:, 128:256] + edge_grad[:, 256:384]
    total = mine - pulled
    for i in range(3):
        forces[i] = total[i : i + 1]


def swap(value, axis, odd):
    count = lax.axis_size(axis)
    pairs = [(i, (((i - odd) ^ 1) + odd) % count) for i in range(count)]
    return lax.ppermute(value, axis, pairs)


def local(
    positions,
    species,
    senders,
    counts,
    owners,
    send_list,
    embedding,
    radial_in_one,
    radial_mid_one,
    radial_out_one,
    mixing,
    square_mix,
    readout_one,
    radial_in_two,
    radial_mid_two,
    radial_out_two,
    mix_two,
    read_hidden,
    read_out,
):
    packed = pl.pallas_call(
        pack_kernel,
        out_shape=jax.ShapeDtypeStruct((16, 128), F32),
        in_specs=[pl.BlockSpec(memory_space=pltpu.HBM)] * 6,
        out_specs=pl.BlockSpec(memory_space=pltpu.VMEM),
        scratch_shapes=[
            pltpu.VMEM((3, 1, 128), F32),
            pltpu.VMEM((1, 128), jnp.int32),
            pltpu.VMEM((3, 1, 128), jnp.int32),
            pltpu.VMEM((1, 128), jnp.int32),
            pltpu.VMEM((3, 1, 128), jnp.int32),
            pltpu.VMEM((1, 64), jnp.int32),
            pltpu.SemaphoreType.DMA((6,)),
        ],
        interpret=INTERPRET,
    )(
        positions.reshape(3, 1, 128),
        species[0],
        senders.reshape(3, 1, 128),
        counts[0],
        owners.reshape(3, 1, 128),
        send_list[0],
    )
    near_a, near_b = swap(packed, "gy", 0), swap(packed, "gy", 1)
    odd_y = lax.axis_index("gy") % 2
    lane = lax.broadcasted_iota(jnp.int32, (16, 128), 1)
    outer = jnp.where(lane // 8 % 2 == odd_y, near_a, near_b)
    mid = jnp.concatenate([packed, outer], 1)
    near_a, near_b = swap(mid, "gx", 0), swap(mid, "gx", 1)
    odd_x = (lax.axis_index("gx") % 2).astype(jnp.int32).reshape(1)
    held = (
        jnp.asarray(ATOM_TABLE),
        jnp.asarray(EDGE_TABLE),
        embedding.T,
        radial_in_one.T,
        radial_mid_one,
        radial_out_one.T,
        mixing,
        square_mix,
        readout_one.reshape(1, -1),
        radial_in_two.T,
        radial_mid_two,
        radial_out_two.T,
        mix_two,
        read_hidden,
        read_out.reshape(1, -1),
    )
    vmem = pl.BlockSpec(memory_space=pltpu.VMEM)
    forces, energies = pl.pallas_call(
        main_kernel,
        out_shape=(
            jax.ShapeDtypeStruct((3, 1, 128), F32),
            jax.ShapeDtypeStruct((1, 128), F32),
        ),
        in_specs=[pl.BlockSpec(memory_space=pltpu.SMEM)]
        + [vmem] * 3
        + [pl.BlockSpec(memory_space=pltpu.HBM)] * len(held),
        out_specs=(vmem, vmem),
        scratch_shapes=[
            pltpu.VMEM((256, 384), BF16),
            pltpu.VMEM((512, 512), BF16),
            pltpu.VMEM((384, 512), BF16),
            pltpu.VMEM((5, 128, 128), F32),
            pltpu.VMEM((8, EDGES), F32),
            pltpu.VMEM((128, EDGES), F32),
            pltpu.VMEM((3, 128, EDGES), F32),
            pltpu.VMEM((16, EDGES), F32),
            pltpu.VMEM((9, 128, 512), F32),
            pltpu.VMEM((128, 512), F32),
            pltpu.VMEM((128, 512), F32),
            pltpu.VMEM((9, 256, 512), BF16),
            pltpu.VMEM((9, 128, EDGES_TWO), F32),
            pltpu.VMEM((3, 128, EDGES_TWO), F32),
            pltpu.VMEM((3, 128, 384), BF16),
            pltpu.VMEM((3, 128, 384), BF16),
            pltpu.VMEM((3, 128, EDGES_TWO), F32),
            pltpu.VMEM((3, 128, EDGES_TWO), F32),
            pltpu.VMEM((128, 256), F32),
            pltpu.VMEM((16, EDGES_BACK), F32),
            pltpu.VMEM((3, 128, EDGES_BACK), F32),
            pltpu.VMEM((4, 64, EDGES_BACK), F32),
            pltpu.VMEM((2, 192, EDGES), BF16),
            pltpu.VMEM((3, 256, EDGES_TWO), BF16),
            pltpu.VMEM((3, 128, 256), F32),
            pltpu.VMEM((3, 128, 256), F32),
            pltpu.VMEM((128, 384), BF16),
        ]
        + [pltpu.VMEM(h.shape, h.dtype) for h in held]
        + [pltpu.SemaphoreType.DMA((len(held),))],
        interpret=INTERPRET,
    )(odd_x, mid, near_a, near_b, *held)
    return forces.reshape(1, 1, 3, 128), energies[None]


def solution(mesh):
    split_four = P("gx", "gy", None, None)
    split_three = P("gx", "gy", None)
    placed = (split_four, split_three, split_four, split_three, split_four, split_three)
    return jax.shard_map(
        local,
        mesh=mesh,
        in_specs=placed + (P(),) * 13,
        out_specs=(split_four, split_three),
        check_vma=False,
    )
```
